256 devices in a mesh: path: 32 (over x, z), mp: 8 (over y, core).
Axes of the slice: x: 4, y: 4, z: 8, core: 2. Of those that a mesh axis runs over, the one named last changes fastest.
Arguments:
- tokens: bfloat16 [12288, 2048], P('path', 'mp'), may hold values from -6 to 6
- cotangent: bfloat16 [12288, 2048], P('path', 'mp'), may hold values from -6 to 6
- path_weights: bfloat16 [32, 3, 4096, 2048], P('path', None, 'mp'), may hold values from -6 to 6
- outer_weights: float32 [32, 3, 8, 8, 16, 2048], P('path', None, None, 'mp'), may hold values from -6 to 6
- momentum: bfloat16 [32, 3, 8, 8, 16, 2048], P('path', None, None, 'mp'), may hold values from -6 to 6
- assignment: int32 [3, 32], replicated, may hold values from 0 to 7, as said below
- owners: int32 [3, 8, 32], replicated, may hold values from 0 to 31, each once within a row
Outputs:
- outputs: bfloat16 [12288, 2048], P('path', 'mp')
- refreshed: bfloat16 [32, 3, 8, 8, 16, 2048], P('path', None, None, 'mp')
The draws below stay inside these ranges and needn't reach their ends.
Inputs may be any that keep to these rules, and one draw needn't show every extreme that they name: `assignment`: every one of the 8 modules of a level is used by at least one path; how many paths share a module varies from module to module. For each level and module, the owners of its 32 pieces are the 32 path indices, each once.
All inputs are finite; a program needn't handle non-finite values.
Results may differ from the reference program's by a relative error of at most 0.0068.
Values may be sent and summed in bfloat16 or wider, within the bound.
A program may use at most 128 MiB of HBM per device.

```python
import jax
import jax.numpy as jnp
from jax import lax

D = 2048
FF = 4096
ROWS = 384
LEVELS = 3
M = 8
TOKENS = 12288
B = 16
N_PATH = 32
N_MP = 8


def draw_assignment(key, part):
    rows = []
    for level in range(LEVELS):
        sub = jax.random.fold_in(key, 11 + level)
        first_key, pick_key, label_key, order_key = jax.random.split(sub, 4)
        first = jax.random.permutation(first_key, M).astype(jnp.int32)
        picks = jax.random.randint(pick_key, (3, N_PATH), 0, M)
        labels = jax.random.permutation(label_key, M).astype(jnp.int32)
        mixed = labels[jnp.min(picks, axis=0)]
        mixed = mixed.at[:M].set(first)
        rows.append(jax.random.permutation(order_key, mixed).astype(jnp.int32))
    return jnp.stack(rows).astype(jnp.int32)


def block_scale(own_key, extent, pieces, least, high):
    level, own = 1.0, jax.random.fold_in(own_key, 6)
    for dim, blocks in pieces:
        heights = jnp.exp(jax.random.uniform(jax.random.fold_in(own, dim), (blocks,), jnp.float32, least / len(pieces), high / len(pieces)))
        level = level * jnp.repeat(heights, extent[dim] // blocks).reshape([-1 if axis == dim else 1 for axis in range(len(extent))])
    return level


def bell_draw(own_key, shape, spread, limit, pieces=(), kind=jnp.bfloat16):
    factor_of = block_scale(own_key, shape, pieces, -0.22, 0.18) if pieces else 1.0
    result = jax.random.normal(own_key, shape, jnp.float32) * spread * factor_of
    return jnp.minimum(jnp.maximum(result, -limit), limit).astype(kind)


def setup_inputs(seed: int = 0) -> dict:
    seeds = jax.random.split(jax.random.key(seed), 8)
    tokens = bell_draw(seeds[0], (TOKENS, D), 1.0, 6.0, ((0, 32), (1, 8)))
    cotangent = bell_draw(seeds[1], (TOKENS, D), 1.0, 6.0, ((0, 32), (1, 8)))
    path_weights = bell_draw(seeds[2], (N_PATH, LEVELS, FF, D), 1.0, 6.0, ((0, 32), (2, 8)))
    outer_weights = bell_draw(seeds[3], (N_PATH, LEVELS, M, N_MP, B, D), 1.0, 6.0, ((0, 32), (3, 8)), jnp.float32)
    momentum = bell_draw(seeds[4], (N_PATH, LEVELS, M, N_MP, B, D), 1.0, 6.0, ((0, 32), (3, 8)))
    assignment = draw_assignment(jax.random.fold_in(seeds[7], 71), 0)
    owners = jax.vmap(lambda own: jax.random.permutation(own, N_PATH))(jax.random.split(seeds[6], LEVELS * M)).reshape((LEVELS, M, N_PATH)).astype(jnp.int32)
    return {"tokens": tokens, "cotangent": cotangent, "path_weights": path_weights, "outer_weights": outer_weights, "momentum": momentum, "assignment": assignment, "owners": owners}


mu_outer = 0.9
eta_outer = 0.7
lr_inner = 2.0


def contract(left, right, left_dim, right_dim):
    return lax.dot_general(left, right, (((left_dim,), (right_dim,)), ((), ())), preferred_element_type=jnp.float32)


def inner_final(inputs, upstream, weights):
    scale_d = D ** -0.5
    scale_f = FF ** -0.5
    gate = contract(inputs, weights[0], 1, 1) * scale_d
    upper = contract(inputs, weights[1], 1, 1) * scale_d
    sig = jax.nn.sigmoid(gate)
    act = gate * sig
    hidden = (act * upper).astype(jnp.bfloat16)
    grad_down = contract(hidden, upstream, 0, 0) * scale_f
    grad_hidden = contract(upstream, weights[2], 1, 1) * scale_f
    pre_gate = (grad_hidden * upper * sig * (1.0 + gate * (1.0 - sig))).astype(jnp.bfloat16)
    pre_up = (grad_hidden * act).astype(jnp.bfloat16)
    grad_gate = contract(pre_gate, inputs, 0, 0) * scale_d
    grad_up = contract(pre_up, inputs, 0, 0) * scale_d
    grads = jnp.stack([grad_gate, grad_up, grad_down])
    return weights.astype(jnp.float32) - lr_inner * grads


def to_full(stored, owner_row):
    placed = stored[owner_row]
    return jnp.transpose(placed, (1, 0, 2, 3)).reshape(FF, D)


def to_owner(full, owner_row):
    blocks = full.reshape(N_MP, N_PATH, -1, D)
    inverse = jnp.argsort(owner_row).astype(jnp.int32)
    return jnp.transpose(blocks[:, inverse], (1, 0, 2, 3))


def reference(tokens, cotangent, path_weights, outer_weights, momentum, assignment, owners):
    level_ids = jnp.arange(LEVELS, dtype=jnp.int32)

    def add_path(total, index):
        inputs = lax.dynamic_slice_in_dim(tokens, index * ROWS, ROWS, 0)
        upstream = lax.dynamic_slice_in_dim(cotangent, index * ROWS, ROWS, 0)
        final = inner_final(inputs, upstream, path_weights[index])
        return total.at[level_ids, assignment[:, index]].add(final), None

    totals, _ = lax.scan(add_path, jnp.zeros((LEVELS, M, FF, D), jnp.float32), jnp.arange(N_PATH, dtype=jnp.int32))
    table = (assignment[:, None, :] == jnp.arange(M, dtype=jnp.int32)[None, :, None]).astype(jnp.float32)
    shares = jnp.sum(table, axis=2)
    full_outer = jax.vmap(jax.vmap(to_full))(jnp.moveaxis(outer_weights, 0, 2), owners)
    full_mom = jax.vmap(jax.vmap(to_full))(jnp.moveaxis(momentum, 0, 2), owners).astype(jnp.float32)
    mean = totals / shares[:, :, None, None]
    delta = full_outer - mean
    velocity = mu_outer * full_mom + delta
    fresh = (full_outer - eta_outer * (delta + mu_outer * velocity)).astype(jnp.bfloat16)
    refreshed = jnp.moveaxis(jax.vmap(jax.vmap(to_owner))(fresh, owners), 2, 0)

    def forward(index):
        inputs = lax.dynamic_slice_in_dim(tokens, index * ROWS, ROWS, 0)
        weights = fresh[level_ids, assignment[:, index]]
        gate = contract(inputs, weights[0], 1, 1) * (D ** -0.5)
        upper = contract(inputs, weights[1], 1, 1) * (D ** -0.5)
        hidden = (gate * jax.nn.sigmoid(gate) * upper).astype(jnp.bfloat16)
        return (contract(hidden, weights[2], 1, 0) * (FF ** -0.5)).astype(jnp.bfloat16)

    outputs = lax.map(forward, jnp.arange(N_PATH, dtype=jnp.int32)).reshape(N_PATH * ROWS, D)
    return outputs, refreshed
```

```python
import jax
import jax.numpy as jnp
from jax import lax
from jax.sharding import PartitionSpec as P

D = 2048
FF = 4096


mu_outer = 0.9
eta_outer = 0.7
lr_inner = 2.0


def contract(left, right, left_dim, right_dim):
    return lax.dot_general(
        left, right, (((left_dim,), (right_dim,)), ((), ())), preferred_element_type=jnp.float32
    )


def shards(tokens, cotangent, path_weights, outer_weights, momentum, assignment, owners):
    inputs, upstream = (
        lax.all_gather(tokens, "mp", axis=1, tiled=True),
        lax.all_gather(cotangent, "mp", axis=1, tiled=True),
    )
    weights = path_weights[0]
    levels = weights.shape[0]
    width = weights.shape[2]
    paths = lax.axis_size("path")
    modules = outer_weights.shape[2]
    block = outer_weights.shape[4]
    scale_d = D ** (-0.5)
    scale_f = FF ** (-0.5)
    level_ids = jnp.arange(levels, dtype=jnp.int32)
    mine = lax.dynamic_index_in_dim(assignment, lax.axis_index("path"), 1, keepdims=False)
    owner_rows = owners[level_ids, mine]
    path_ids = jnp.arange(paths, dtype=jnp.int32)
    inverse = jnp.sum(
        path_ids[None, :, None]
        * (owner_rows[:, :, None] == path_ids[None, None, :]).astype(jnp.int32),
        axis=1,
    )
    table = (assignment[:, None, :] == jnp.arange(modules, dtype=jnp.int32)[None, :, None]).astype(
        jnp.float32
    )
    shares = jnp.sum(table, axis=2)
    stored = outer_weights[0, :, :, 0]
    velocity_old = momentum[0, :, :, 0].astype(jnp.float32)
    gate = contract(inputs, weights[0], 1, 1) * scale_d
    upper = contract(inputs, weights[1], 1, 1) * scale_d
    sig = jax.nn.sigmoid(gate)
    act = gate * sig
    hidden = (act * upper).astype(jnp.bfloat16)
    grad_hidden = contract(upstream, weights[2], 1, 1) * scale_f
    pre_gate = (grad_hidden * upper * sig * (1.0 + gate * (1.0 - sig))).astype(jnp.bfloat16)
    pre_up = (grad_hidden * act).astype(jnp.bfloat16)

    def final_level(level):
        if level == 2:
            grad = contract(hidden, upstream, 0, 0) * scale_f
        elif level == 0:
            grad = contract(pre_gate, inputs, 0, 0) * scale_d
        else:
            grad = contract(pre_up, inputs, 0, 0) * scale_d
        return (weights[level].astype(jnp.float32) - lr_inner * grad).astype(jnp.bfloat16)

    finals = jnp.stack([final_level(0), final_level(1), final_level(2)])
    count = finals.shape[0]
    blocks = finals.reshape(count, paths, block, width)
    received = lax.all_to_all(
        blocks[jnp.arange(count)[:, None], inverse], "path", split_axis=1, concat_axis=1, tiled=True
    )
    count = received.shape[0]
    sums = jnp.einsum(
        "lmp,lpbd->lmbd", table.astype(jnp.bfloat16), received, preferred_element_type=jnp.float32
    )
    mean = sums / shares[0 : 0 + count, :, None, None]
    delta = stored - mean
    velocity = mu_outer * velocity_old + delta
    fresh = (stored - eta_outer * (delta + mu_outer * velocity)).astype(jnp.bfloat16)
    fresh, leaving = (fresh, fresh[jnp.arange(count)[:, None], assignment])
    returned = lax.all_to_all(leaving, "path", split_axis=1, concat_axis=1, tiled=True)
    count = returned.shape[0]
    placed = returned[jnp.arange(count)[:, None], owner_rows]
    new_weights = placed.reshape(count, paths * block, width)
    gate_new = contract(inputs, new_weights[0], 1, 1) * scale_d
    upper_new = contract(inputs, new_weights[1], 1, 1) * scale_d
    hidden_new = (gate_new * jax.nn.sigmoid(gate_new) * upper_new).astype(jnp.bfloat16)
    partial_out = contract(hidden_new, new_weights[2], 1, 0) * scale_f
    mp = lax.axis_size("mp")
    rows = partial_out.shape[0]
    slices = partial_out.astype(jnp.bfloat16).reshape(rows, mp, -1).swapaxes(0, 1)
    arrived = lax.all_to_all(slices, "mp", split_axis=0, concat_axis=0, tiled=True)
    outputs = jnp.sum(arrived.astype(jnp.float32), axis=0).astype(jnp.bfloat16)
    refreshed = fresh.reshape(1, levels, modules, 1, block, width)
    return (outputs, refreshed)


def solution(mesh):
    return jax.shard_map(
        shards,
        mesh=mesh,
        in_specs=(
            P("path", "mp"),
            P("path", "mp"),
            P("path", None, "mp", None),
            P("path", None, None, "mp", None, None),
            P("path", None, None, "mp", None, None),
            P(),
            P(),
        ),
        out_specs=(P("path", "mp"), P("path", None, None, "mp", None, None)),
        check_vma=False,
    )
```

```python
import jax
import jax.numpy as jnp
from jax import lax
from jax.experimental import pallas as pl
from jax.experimental.pallas import tpu as pltpu
from jax.sharding import PartitionSpec as P

MESH = pl.DeviceIdType.MESH

D = 2048
FF = 4096


mu_outer = 0.9
eta_outer = 0.7
lr_inner = 2.0

NX = 4
NZ = 8
KORD = (4, 3, 5, 2, 6, 1, 7, 0)
POS = {k: i for i, k in enumerate(KORD)}
GROUPS = ((0, 1), (1, 3), (3, 5), (5, 7), (7, 8))
M = 8
LV = 3
B = 16
HALF = D // 2
CH = 256
SIGN = (-1, 1)


def exchange_kernel(
    mask, pick, rcp, finals, outer, momentum, returned, refreshed, *scratch
):
    it = iter(scratch)
    take = lambda n: [next(it) for _ in range(n)]
    pairs = lambda: [take(2) for _ in range(LV)]
    X = take(LV)
    B0, B1o, B1f, T2, B2, B3 = (pairs() for _ in range(6))
    F = take(LV)
    C1, C2, C3d, S2, C3s, S3, C4 = (pairs() for _ in range(7))
    Y = take(LV)
    O, V = take(LV), take(LV)
    xs, xr, zs, zr, ls = take(5)
    me = lax.axis_index("path")
    x, z = me // NZ, lax.rem(me, NZ)
    right = [lax.rem(x + dx, NX) * NZ + z for dx in range(NX)]
    along = [x * NZ + lax.rem(z + NZ + s, NZ) for s in SIGN]

    barrier = pltpu.get_barrier_semaphore()
    for other in right[1:] + along:
        pl.semaphore_signal(barrier, inc=1, device_id={"path": other}, device_id_type=MESH)
    pl.semaphore_wait(barrier, 5)

    started = []
    zc = {}
    xc = {}

    def local(key, src, dst, index):
        c = pltpu.make_async_copy(src, dst, ls.at[index])
        c.start()
        xc[key] = c

    def remote(table, key, src, dst, ssem, rsem, other):
        c = pltpu.make_async_remote_copy(
            src_ref=src, dst_ref=dst, send_sem=ssem, recv_sem=rsem,
            device_id={"path": other}, device_id_type=MESH,
        )
        c.start()
        started.append(c)
        table[key] = c

    def zsend(l, s, step, src, dst):
        remote(zc, (l, s, step), src, dst, zs.at[l, s, step], zr.at[l, s, step], along[s])

    def zwait(l, s, step):
        zc[l, s, step].wait_recv()

    def xwait(l, g):
        for dx in range(1, NX):
            xc[l, g, dx].wait_recv()

    def combine(dst, bases, terms, lo, hi):
        def body(c, carry):
            col = pl.multiple_of(lo + c * CH, CH)
            vals = [
                (ref[idx, :, pl.ds(pl.multiple_of(col - off, CH), CH)].astype(jnp.float32), at)
                for ref, idx, off, at in terms
            ]
            for m in range(M):
                acc = None
                for base in bases:
                    v = base[m, :, pl.ds(col, CH)].astype(jnp.float32)
                    acc = v if acc is None else acc + v
                for v, at in vals:
                    t = v * mask[at + m]
                    acc = t if acc is None else acc + t
                dst(m, col, acc)
            return carry

        lax.fori_loop(0, (hi - lo) // CH, body, 0)

    def at(l, j, r):
        return ((l * NZ + j % NZ) * NX + r) * M

    def own(l, k):
        return [(X[l].at[POS[k % NZ]], r, 0, at(l, 0, r)) for r in range(NX)]

    def into(ref):
        def put(m, col, acc):
            ref[m, :, pl.ds(col, CH)] = acc.astype(jnp.bfloat16)
        return put

    def a0(l):
        if l == 0:
            for i in range(LV):
                local(("o", i), outer.at[i], O[i], 6 + i)
                local(("v", i), momentum.at[i], V[i], 9 + i)
        local((l, "own"), finals.at[l, 0], X[l].at[:, 0], l)
        for g, (lo, hi) in enumerate(GROUPS):
            for dx in (1, 3, 2):
                remote(
                    xc, (l, g, dx), finals.at[l, dx, pl.ds(lo, hi - lo)],
                    X[l].at[pl.ds(lo, hi - lo), dx], xs.at[0, l, g, dx - 1], xr.at[0, l, g, dx - 1],
                    right[dx],
                )

    def a1(l):
        xc[l, "own"].wait()
        xwait(l, 0)
        for s in (0, 1):
            zsend(l, s, 0, X[l].at[0, :, :, pl.ds(s * HALF, HALF)], B0[l][s])

    def a2(l):
        xwait(l, 1)
        for s in (0, 1):
            zsend(l, s, 1, X[l].at[POS[3 * SIGN[s] % NZ]], B1o[l][s])
        for s in (0, 1):
            zwait(l, s, 0)
            zsend(l, s, 2, B0[l][s], B1f[l][s])

    def a3(l):
        xwait(l, 2)
        for s in (0, 1):
            sg = SIGN[s]
            zwait(l, s, 1)
            near = own(l, 2 * sg) + [(B1o[l][s], r, 0, at(l, -sg, r)) for r in range(NX)]
            o = (1 - s) * HALF
            combine(into(T2[l][s]), [], near, o, o + HALF)
            zwait(l, s, 2)
            o = s * HALF
            far = [(B1f[l][s], r, o, at(l, -2 * sg, r)) for r in range(NX)]
            combine(into(T2[l][s]), [], near + far, o, o + HALF)
            zsend(l, s, 3, T2[l][s], B2[l][s])

    def a4(l):
        xwait(l, 3)
        for s in (0, 1):
            zwait(l, s, 3)
            combine(into(B2[l][s]), [B2[l][s]], own(l, SIGN[s]), 0, D)
            zsend(l, s, 4, B2[l][s], B3[l][s])

    def stage(l, k, src):
        i = POS[k % NZ]
        for dx in range(NX):
            src(i, dx, pick[(l * NZ) * NX + dx])

    def xsend(l, g):
        lo, hi = GROUPS[g]
        n = hi - lo
        for dx in (1, 3, 2):
            remote(
                xc, (l, g, dx, "r"), Y[l].at[dx, pl.ds(lo, n)], returned.at[l, dx, pl.ds(lo, n)],
                xs.at[1, l, g, dx - 1], xr.at[1, l, g, dx - 1], right[dx],
            )

    def a5(l):
        xwait(l, 4)
        xc["o", l].wait()
        xc["v", l].wait()
        for s in (0, 1):
            zwait(l, s, 4)

        def put(m, col, acc):
            cols = pl.ds(col, CH)
            stored = O[l][m, :, cols]
            delta = stored - acc * rcp[l * M + m]
            velocity = mu_outer * V[l][m, :, cols].astype(jnp.float32) + delta
            F[l][m, :, cols] = (stored - eta_outer * (delta + mu_outer * velocity)).astype(jnp.bfloat16)

        combine(put, [B3[l][0], B3[l][1]], own(l, 0), 0, D)
        for s in (0, 1):
            zsend(l, s, 5, F[l], C1[l][s])
        local((l, "fresh"), F[l], refreshed.at[l], 3 + l)

        def src(i, dx, a):
            Y[l][dx, i] = F[l][a]

        stage(l, 0, src)
        xsend(l, 4)

    def a6(l):
        for s in (0, 1):
            zwait(l, s, 5)
            zsend(l, s, 6, C1[l][s], C2[l][s])
        for s in (0, 1):
            def src(i, dx, a):
                Y[l][dx, i] = C1[l][s][a]

            stage(l, -SIGN[s], src)
        xsend(l, 3)

    def a7(l):
        for s in (0, 1):
            zwait(l, s, 6)
            zsend(l, s, 7, C2[l][s].at[:, :, pl.ds(s * HALF, HALF)], C3d[l][s])
            j = SIGN[s] % NZ
            for dx in range(NX):
                a = pick[(l * NZ + j) * NX + dx]
                S2[l][s][dx] = C2[l][s][a, :, pl.ds((1 - s) * HALF, HALF)]
            zsend(l, s, 8, S2[l][s], C3s[l][s])
        for s in (0, 1):
            def src(i, dx, a):
                Y[l][dx, i] = C2[l][s][a]

            stage(l, -2 * SIGN[s], src)
        xsend(l, 2)

    def a8(l):
        for s in (0, 1):
            zwait(l, s, 7)
            j = SIGN[s] % NZ
            for dx in range(NX):
                a = pick[(l * NZ + j) * NX + dx]
                S3[l][s][dx] = C3d[l][s][a]
            zsend(l, s, 9, S3[l][s], C4[l][s])
        for s in (0, 1):
            zwait(l, s, 8)

            def src(i, dx, a):
                Y[l][dx, i, :, pl.ds(s * HALF, HALF)] = C3d[l][s][a]
                Y[l][dx, i, :, pl.ds((1 - s) * HALF, HALF)] = C3s[l][s][dx]

            stage(l, -3 * SIGN[s], src)
        xsend(l, 1)

    def a9(l):
        for s in (0, 1):
            zwait(l, s, 9)
        def src(i, dx, a):
            for s in (0, 1):
                Y[l][dx, i, :, pl.ds(s * HALF, HALF)] = C4[l][s][dx]

        stage(l, 4, src)
        xsend(l, 0)
        local((l, "mine"), Y[l].at[0], returned.at[l, 0], 12 + l)

    def a10(l):
        for g in range(len(GROUPS)):
            for dx in range(1, NX):
                xc[l, g, dx, "r"].wait_recv()
        xc[l, "mine"].wait()
        xc[l, "fresh"].wait()

    steps = (a0, a1, a2, a3, a4, a5, a6, a7, a8, a9, a10)
    for slot in range(len(steps) + (LV - 1)):
        for l in range(LV):
            if 0 <= slot - l < len(steps):
                steps[slot - l](l)
    for c in started:
        c.wait_send()


def exchange(mask, pick, rcp, finals, outer, momentum):
    bf = lambda *shape: pltpu.VMEM(shape, jnp.bfloat16)
    full, half = (D,), (HALF,)
    dense, dense_half = bf(M, B, D), bf(M, B, HALF)
    four, four_half = bf(NX, B, D), bf(NX, B, HALF)
    pairs = lambda kind: [kind] * (2 * LV)
    scratch = [bf(NZ, NX, B, D)] * LV
    for kind in (four_half, four, four_half, dense, dense, dense):
        scratch += pairs(kind)
    scratch += [dense] * LV
    for kind in (dense, dense, dense_half, four_half, four_half, four_half, four_half):
        scratch += pairs(kind)
    scratch += [bf(NX, NZ, B, D)] * LV
    scratch += [pltpu.VMEM((M, B, D), jnp.float32)] * LV + [dense] * LV
    dma = pltpu.SemaphoreType.DMA
    scratch += [dma((2, LV, 5, 3)), dma((2, LV, 5, 3)), dma((LV, 2, 10)), dma((LV, 2, 10)), dma((15,))]
    smem = pl.BlockSpec(memory_space=pltpu.SMEM)
    anyw = pl.BlockSpec(memory_space=pl.ANY)
    return pl.pallas_call(
        exchange_kernel,
        out_shape=(
            jax.ShapeDtypeStruct((LV, NX, NZ, B, D), jnp.bfloat16),
            jax.ShapeDtypeStruct((LV, M, B, D), jnp.bfloat16),
        ),
        in_specs=[smem, smem, smem, anyw, anyw, anyw],
        out_specs=(anyw, anyw),
        scratch_shapes=scratch,
        compiler_params=pltpu.CompilerParams(
            collective_id=0, has_side_effects=True, vmem_limit_bytes=62 * 1024 * 1024
        ),
    )(mask, pick, rcp, finals, outer, momentum)


def contract(left, right, left_dim, right_dim):
    return lax.dot_general(
        left, right, (((left_dim,), (right_dim,)), ((), ())), preferred_element_type=jnp.float32
    )


def shards(tokens, cotangent, path_weights, outer_weights, momentum, assignment, owners):
    inputs, upstream = (
        lax.all_gather(tokens, "mp", axis=1, tiled=True),
        lax.all_gather(cotangent, "mp", axis=1, tiled=True),
    )
    weights = path_weights[0]
    levels = weights.shape[0]
    width = weights.shape[2]
    paths = lax.axis_size("path")
    modules = outer_weights.shape[2]
    block = outer_weights.shape[4]
    scale_d = D ** (-0.5)
    scale_f = FF ** (-0.5)
    level_ids = jnp.arange(levels, dtype=jnp.int32)
    mine = lax.dynamic_index_in_dim(assignment, lax.axis_index("path"), 1, keepdims=False)
    owner_rows = owners[level_ids, mine]
    path_ids = jnp.arange(paths, dtype=jnp.int32)
    inverse = jnp.sum(
        path_ids[None, :, None]
        * (owner_rows[:, :, None] == path_ids[None, None, :]).astype(jnp.int32),
        axis=1,
    )
    here = lax.axis_index("path")
    at_x, at_z = here // NZ, here % NZ
    kord = jnp.array(KORD, dtype=jnp.int32)
    xs, zs = jnp.arange(NX, dtype=jnp.int32), jnp.arange(NZ, dtype=jnp.int32)
    ahead = ((at_x + xs) % NX)[:, None] * NZ + ((at_z + kord) % NZ)[None, :]
    behind = ((at_x - xs) % NX)[:, None] * NZ + ((at_z + kord) % NZ)[None, :]
    rows_z = (at_z + zs) % NZ
    from_ids = ((at_x - xs) % NX)[None, :] * NZ + rows_z[:, None]
    to_ids = ((at_x + xs) % NX)[None, :] * NZ + rows_z[:, None]
    module_ids = jnp.arange(modules, dtype=jnp.int32)
    mask = (assignment[:, from_ids][..., None] == module_ids).astype(jnp.float32).reshape(-1)
    pick = assignment[:, to_ids].reshape(-1)
    shares = jnp.sum((assignment[:, :, None] == module_ids).astype(jnp.float32), axis=1)
    rcp = (1.0 / shares).reshape(-1)
    gate = contract(inputs, weights[0], 1, 1) * scale_d
    upper = contract(inputs, weights[1], 1, 1) * scale_d
    sig = jax.nn.sigmoid(gate)
    act = gate * sig
    hidden = (act * upper).astype(jnp.bfloat16)
    grad_hidden = contract(upstream, weights[2], 1, 1) * scale_f
    pre_gate = (grad_hidden * upper * sig * (1.0 + gate * (1.0 - sig))).astype(jnp.bfloat16)
    pre_up = (grad_hidden * act).astype(jnp.bfloat16)

    def final_level(level):
        if level == 2:
            grad = contract(hidden, upstream, 0, 0) * scale_f
        elif level == 0:
            grad = contract(pre_gate, inputs, 0, 0) * scale_d
        else:
            grad = contract(pre_up, inputs, 0, 0) * scale_d
        return (weights[level].astype(jnp.float32) - lr_inner * grad).astype(jnp.bfloat16)

    finals = jnp.stack([final_level(0), final_level(1), final_level(2)])
    count = finals.shape[0]
    blocks = finals.reshape(count, paths, block, width)
    leaving = blocks[level_ids[:, None], inverse[:, ahead.reshape(-1)]]
    returned, fresh = exchange(
        mask,
        pick,
        rcp,
        leaving.reshape(count, NX, NZ, block, width),
        outer_weights.reshape(count, modules, block, width),
        momentum.reshape(count, modules, block, width),
    )
    slot_of = jnp.sum(
        jnp.where(behind.reshape(-1)[None, :] == path_ids[:, None], path_ids[None, :], 0), axis=1
    )
    placed = returned.reshape(count, paths, block, width)[
        level_ids[:, None], slot_of[owner_rows]
    ]
    new_weights = placed.reshape(count, paths * block, width)
    gate_new = contract(inputs, new_weights[0], 1, 1) * scale_d
    upper_new = contract(inputs, new_weights[1], 1, 1) * scale_d
    hidden_new = (gate_new * jax.nn.sigmoid(gate_new) * upper_new).astype(jnp.bfloat16)
    partial_out = contract(hidden_new, new_weights[2], 1, 0) * scale_f
    mp = lax.axis_size("mp")
    rows = partial_out.shape[0]
    slices = partial_out.astype(jnp.bfloat16).reshape(rows, mp, -1).swapaxes(0, 1)
    arrived = lax.all_to_all(slices, "mp", split_axis=0, concat_axis=0, tiled=True)
    outputs = jnp.sum(arrived.astype(jnp.float32), axis=0).astype(jnp.bfloat16)
    refreshed = fresh.reshape(1, levels, modules, 1, block, width)
    return (outputs, refreshed)


def solution(mesh):
    return jax.shard_map(
        shards,
        mesh=mesh,
        in_specs=(
            P("path", "mp"),
            P("path", "mp"),
            P("path", None, "mp", None),
            P("path", None, None, "mp", None, None),
            P("path", None, None, "mp", None, None),
            P(),
            P(),
        ),
        out_specs=(P("path", "mp"), P("path", None, None, "mp", None, None)),
        check_vma=False,
    )
```

```python
import jax
import jax.numpy as jnp
from jax import lax
from jax.experimental import pallas as pl
from jax.experimental.pallas import tpu as pltpu
from jax.sharding import PartitionSpec as P

MESH = pl.DeviceIdType.MESH
D = 2048
FF = 4096
ROWS = 384
NX = 4
NZ = 8
NY = 4
NP = NX * NZ
NMP = 8
PART = D // NMP
KORD = (4, 3, 5, 2, 6, 1, 7, 0)
POS = {k: i for i, k in enumerate(KORD)}
GROUPS = ((0, 1), (1, 3), (3, 5), (5, 7), (7, 8))
M = 8
LV = 3
B = 16
HID = NP * B
HALF = D // 2
HROW = ROWS // 2
CH = 256
SIGN = (-1, 1)

mu_outer = 0.9
eta_outer = 0.7
lr_inner = 2.0
scale_d = D ** (-0.5)
scale_f = FF ** (-0.5)
f32 = jnp.float32
bf16 = jnp.bfloat16


def contract(left, right, left_dim, right_dim):
    return lax.dot_general(
        left, right, (((left_dim,), (right_dim,)), ((), ())), preferred_element_type=f32
    )


def step_kernel(
    assign, table, rcp, tokens, cotangent, weights, outer, momentum, out, refreshed, *scratch
):
    it = iter(scratch)
    take = lambda n: [next(it) for _ in range(n)]
    pairs = lambda: [take(2) for _ in range(LV)]
    X = take(LV)
    B0, B1o, B1f, T2, B2, B3 = (pairs() for _ in range(6))
    C1, C2, C3d, S2, C3s, S3, C4 = (pairs() for _ in range(7))
    Y, WR, O, F = take(LV), take(LV), take(LV), take(LV)
    xg, cg = take(2)
    A0, A1, A2 = take(3)
    hid, pre0, pre1, perm, G, h2 = take(6)
    N0, NS, NR, TS2, TE, TS1, TR = take(7)
    mask = next(it)
    xs, xr, zs, zr, ls, gs, gr, ts, tr = take(9)
    me = lax.axis_index("path")
    mp = lax.axis_index("mp")
    x, z = me // NZ, lax.rem(me, NZ)
    y, core = mp // 2, lax.rem(mp, 2)
    right = [lax.rem(x + dx, NX) * NZ + z for dx in range(NX)]
    along = [x * NZ + lax.rem(z + NZ + s, NZ) for s in SIGN]
    ycol = lambda dy: lax.rem(y + dy + NY, NY) * 2 + core
    up, down, mate = ycol(1), ycol(-1), y * 2 + 1 - core

    barrier = pltpu.get_barrier_semaphore()
    for other in right[1:] + along:
        pl.semaphore_signal(barrier, inc=1, device_id={"path": other}, device_id_type=MESH)
    for other in (up, down, mate):
        pl.semaphore_signal(barrier, inc=1, device_id={"mp": other}, device_id_type=MESH)

    started, zc, xc, loc = [], {}, {}, {}

    def local(key, src, dst, index):
        c = pltpu.make_async_copy(src, dst, ls.at[index])
        c.start()
        loc[key] = c

    def describe(src, dst, ssem, rsem, axis, other):
        return pltpu.make_async_remote_copy(
            src_ref=src, dst_ref=dst, send_sem=ssem, recv_sem=rsem,
            device_id={axis: other}, device_id_type=MESH,
        )

    def remote(key, keep, *rest):
        c = describe(*rest)
        c.start()
        started.append(c)
        keep[key] = c

    local("xg", tokens, xg.at[mp], 15)
    local("cg", cotangent, cg.at[mp], 16)
    for l in range(LV):
        local(("w", l), weights.at[l], WR[l], 12 + l)
        local(("o", l), outer.at[l], O[l], 6 + l)
        local(("v", l), momentum.at[l], F[l], 9 + l)
    pl.semaphore_wait(barrier, 8)

    def gsend(t, n, src, dst, other):
        remote(("g", t, n), zc, src, dst, gs.at[t, n], gr.at[t, n], "mp", other)

    def gwait(t, n, dst):
        describe(dst, dst, gs.at[t, n], gr.at[t, n], "mp", mate).wait_recv()

    both = ((tokens, xg), (cotangent, cg))
    first, second = pl.ds(0, HROW), pl.ds(HROW, HROW)
    for t, (src, g) in enumerate(both):
        gsend(t, 0, src, g.at[mp], up)
        gsend(t, 1, src, g.at[mp], down)
        gsend(t, 2, src, g.at[mp], mate)

    def masks(i, carry):
        l, rest = i // (NZ * NX), lax.rem(i, NZ * NX)
        j, r = rest // NX, lax.rem(rest, NX)
        a = assign[l * NP + lax.rem(x - r + NX, NX) * NZ + lax.rem(z + j, NZ)]
        for m in range(M):
            mask[i * M + m] = jnp.where(a == m, 1.0, 0.0).astype(f32)
        return carry

    lax.fori_loop(0, LV * NZ * NX, masks, 0)

    def relay(t):
        g = both[t][1]
        lo, hi, far = ycol(-1), ycol(1), ycol(2)
        gwait(t, 0, g.at[lo])
        gsend(t, 3, g.at[lo, first], g.at[lo, first], up)
        gsend(t, 4, g.at[lo], g.at[lo], mate)
        gwait(t, 1, g.at[hi])
        gsend(t, 5, g.at[hi, second], g.at[hi, second], down)
        gsend(t, 6, g.at[hi], g.at[hi], mate)
        gwait(t, 3, g.at[far, first])
        gwait(t, 5, g.at[far, second])
        gsend(t, 7, g.at[far], g.at[far], mate)

    def arrived(t):
        g = both[t][1]
        other = lambda dy: lax.rem(y + dy, NY) * 2 + 1 - core
        gwait(t, 2, g.at[other(0)])
        gwait(t, 4, g.at[other(3)])
        gwait(t, 6, g.at[other(1)])
        gwait(t, 7, g.at[other(2)])
        loc["xg" if t == 0 else "cg"].wait()

    def project(jobs, g):
        def body(j, carry):
            cols = pl.ds(pl.multiple_of(j * PART, PART), PART)
            for acc, w in jobs:
                part = contract(w[:, :, cols].reshape(HID, PART), g[j], 1, 1)
                acc[...] += part.reshape(NP, B, ROWS)
            return carry

        for acc, _ in jobs:
            acc[...] = jnp.zeros_like(acc)
        lax.fori_loop(0, NMP, body, 0)

    relay(0)
    loc["w", 0].wait()
    loc["w", 1].wait()
    loc["w", 2].wait()
    arrived(0)
    relay(1)
    project(((A0, WR[0]), (A1, WR[1])), xg)
    arrived(1)
    project(((A2, WR[2]),), cg)

    def nonlinear(i, carry):
        gate, upper, back = A0[i] * scale_d, A1[i] * scale_d, A2[i] * scale_f
        sig = jax.nn.sigmoid(gate)
        act = gate * sig
        hid[i] = (act * upper).astype(bf16)
        pre0[i] = (back * upper * sig * (1.0 + gate * (1.0 - sig))).astype(bf16)
        pre1[i] = (back * act).astype(bf16)
        return carry

    lax.fori_loop(0, NP, nonlinear, 0)

    def finals(l):
        left = (pre0, pre1, hid)[l]
        g = (xg, xg, cg)[l]
        rate = lr_inner * (scale_d, scale_d, scale_f)[l]

        def gather(s, carry):
            perm[s] = left[table[l * NP + s]]
            return carry

        lax.fori_loop(0, NP, gather, 0, unroll=4)

        def body(j, carry):
            cols = pl.ds(pl.multiple_of(j * PART, PART), PART)
            G[...] = contract(perm[...].reshape(HID, ROWS), g[j], 1, 0).reshape(NP, B, PART)

            def rows(s, inner):
                w = WR[l][table[l * NP + s], :, cols].astype(f32)
                Y[l][s, :, cols] = (w - rate * G[s]).astype(bf16)
                return inner

            return lax.fori_loop(0, NP, rows, carry, unroll=8)

        lax.fori_loop(0, NMP, body, 0)

    def zsend(l, s, step, src, dst):
        remote(
            (l, s, step), zc, src, dst, zs.at[l, s, step], zr.at[l, s, step], "path", along[s]
        )

    def zwait(l, s, step):
        zc[l, s, step].wait_recv()

    def xwait(l, g):
        for dx in range(1, NX):
            xc[l, g, dx].wait_recv()

    def combine(dst, bases, terms, lo, hi):
        def body(c, carry):
            col = pl.multiple_of(lo + c * CH, CH)
            vals = [
                (ref[idx, :, pl.ds(pl.multiple_of(col - off, CH), CH)].astype(f32), at)
                for ref, idx, off, at in terms
            ]
            for m in range(M):
                acc = None
                for base in bases:
                    v = base[m, :, pl.ds(col, CH)].astype(f32)
                    acc = v if acc is None else acc + v
                for v, at in vals:
                    t = v * mask[at + m]
                    acc = t if acc is None else acc + t
                dst(m, col, acc)
            return carry

        lax.fori_loop(0, (hi - lo) // CH, body, 0)

    def at(l, j, r):
        return ((l * NZ + j % NZ) * NX + r) * M

    def own(l, k):
        return [(X[l].at[POS[k % NZ]], r, 0, at(l, 0, r)) for r in range(NX)]

    def into(ref):
        def put(m, col, acc):
            ref[m, :, pl.ds(col, CH)] = acc.astype(bf16)
        return put

    def pick(l, j, dx):
        return assign[l * NP + lax.rem(x + dx, NX) * NZ + lax.rem(z + j % NZ, NZ)]

    def a0(l):
        local((l, "own"), Y[l].at[pl.ds(0, NZ)], X[l].at[:, 0], l)
        for g, (lo, hi) in enumerate(GROUPS):
            for dx in (1, 3, 2):
                remote(
                    (l, g, dx), xc, Y[l].at[pl.ds(dx * NZ + lo, hi - lo)],
                    X[l].at[pl.ds(lo, hi - lo), dx], xs.at[0, l, g, dx - 1], xr.at[0, l, g, dx - 1],
                    "path", right[dx],
                )

    def a1(l):
        loc[l, "own"].wait()
        xwait(l, 0)
        for s in (0, 1):
            zsend(l, s, 0, X[l].at[0, :, :, pl.ds(s * HALF, HALF)], B0[l][s])

    def a2(l):
        xwait(l, 1)
        for s in (0, 1):
            zsend(l, s, 1, X[l].at[POS[3 * SIGN[s] % NZ]], B1o[l][s])
        for s in (0, 1):
            zwait(l, s, 0)
            zsend(l, s, 2, B0[l][s], B1f[l][s])

    def a3(l):
        xwait(l, 2)
        for s in (0, 1):
            sg = SIGN[s]
            zwait(l, s, 1)
            near = own(l, 2 * sg) + [(B1o[l][s], r, 0, at(l, -sg, r)) for r in range(NX)]
            o = (1 - s) * HALF
            combine(into(T2[l][s]), [], near, o, o + HALF)
            zwait(l, s, 2)
            o = s * HALF
            far = [(B1f[l][s], r, o, at(l, -2 * sg, r)) for r in range(NX)]
            combine(into(T2[l][s]), [], near + far, o, o + HALF)
            zsend(l, s, 3, T2[l][s], B2[l][s])

    def a4(l):
        xwait(l, 3)
        for s in (0, 1):
            zwait(l, s, 3)
            combine(into(B2[l][s]), [B2[l][s]], own(l, SIGN[s]), 0, D)
            zsend(l, s, 4, B2[l][s], B3[l][s])

    def stage(l, k, src):
        i = POS[k % NZ]
        for dx in range(NX):
            src(dx * NZ + i, dx, pick(l, 0, dx))

    def xsend(l, g):
        lo, hi = GROUPS[g]
        n = hi - lo
        for dx in (1, 3, 2):
            part = pl.ds(dx * NZ + lo, n)
            remote(
                (l, g, dx, "r"), xc, Y[l].at[part], WR[l].at[part],
                xs.at[1, l, g, dx - 1], xr.at[1, l, g, dx - 1], "path", right[dx],
            )

    def a5(l):
        xwait(l, 4)
        loc["o", l].wait()
        loc["v", l].wait()
        for s in (0, 1):
            zwait(l, s, 4)

        def put(m, col, acc):
            cols = pl.ds(col, CH)
            stored = O[l][m, :, cols]
            delta = stored - acc * rcp[l * M + m]
            velocity = mu_outer * F[l][m, :, cols].astype(f32) + delta
            F[l][m, :, cols] = (stored - eta_outer * (delta + mu_outer * velocity)).astype(bf16)

        combine(put, [B3[l][0], B3[l][1]], own(l, 0), 0, D)
        for s in (0, 1):
            zsend(l, s, 5, F[l], C1[l][s])
        local((l, "fresh"), F[l], refreshed.at[l], 3 + l)
        for g in range(len(GROUPS)):
            for dx in range(1, NX):
                xc[l, g, dx].wait_send()

        def src(i, dx, a):
            Y[l][i] = F[l][a]

        stage(l, 0, src)
        xsend(l, 4)

    def a6(l):
        for s in (0, 1):
            zwait(l, s, 5)
            zsend(l, s, 6, C1[l][s], C2[l][s])
        for s in (0, 1):
            def src(i, dx, a):
                Y[l][i] = C1[l][s][a]

            stage(l, -SIGN[s], src)
        xsend(l, 3)

    def a7(l):
        for s in (0, 1):
            zwait(l, s, 6)
            zsend(l, s, 7, C2[l][s].at[:, :, pl.ds(s * HALF, HALF)], C3d[l][s])
            for dx in range(NX):
                S2[l][s][dx] = C2[l][s][pick(l, SIGN[s], dx), :, pl.ds((1 - s) * HALF, HALF)]
            zsend(l, s, 8, S2[l][s], C3s[l][s])
        for s in (0, 1):
            def src(i, dx, a):
                Y[l][i] = C2[l][s][a]

            stage(l, -2 * SIGN[s], src)
        xsend(l, 2)

    def a8(l):
        for s in (0, 1):
            zwait(l, s, 7)
            for dx in range(NX):
                S3[l][s][dx] = C3d[l][s][pick(l, SIGN[s], dx)]
            zsend(l, s, 9, S3[l][s], C4[l][s])
        for s in (0, 1):
            zwait(l, s, 8)

            def src(i, dx, a):
                Y[l][i, :, pl.ds(s * HALF, HALF)] = C3d[l][s][a]
                Y[l][i, :, pl.ds((1 - s) * HALF, HALF)] = C3s[l][s][dx]

            stage(l, -3 * SIGN[s], src)
        xsend(l, 1)

    def a9(l):
        for s in (0, 1):
            zwait(l, s, 9)

        def src(i, dx, a):
            for s in (0, 1):
                Y[l][i, :, pl.ds(s * HALF, HALF)] = C4[l][s][dx]

        stage(l, 4, src)
        xsend(l, 0)
        local((l, "mine"), Y[l].at[pl.ds(0, NZ)], WR[l].at[pl.ds(0, NZ)], 17 + l)

    def settle(l):
        for g in range(len(GROUPS)):
            for dx in range(1, NX):
                xc[l, g, dx, "r"].wait_recv()
        loc[l, "mine"].wait()

    def forward(l):
        settle(l)
        if l < 2:
            project((((A0, A1)[l], WR[l]),), xg)
        if l == 1:
            def body(s, carry):
                gate = A0[table[LV * NP + s]] * scale_d
                upper = A1[table[(LV + 1) * NP + s]] * scale_d
                A2[s] = gate * jax.nn.sigmoid(gate) * upper
                return carry

            lax.fori_loop(0, NP, body, 0)
            h2[...] = A2[...].reshape(HID, ROWS).T.astype(bf16)

    finals(0)
    a0(0)
    finals(1)
    steps = (a0, a1, a2, a3, a4, a5, a6, a7, a8, a9)
    for slot in range(1, len(steps) + LV - 1):
        for l in range(LV):
            if 0 <= slot - l < len(steps):
                steps[slot - l](l)
        if slot == 1:
            finals(2)
        if slot >= len(steps):
            forward(slot - len(steps))
    settle(2)

    def block(j):
        cols = pl.ds(pl.multiple_of(j * PART, PART), PART)
        return contract(h2[...], WR[2][:, :, cols].reshape(HID, PART), 1, 0) * scale_f

    def tsend(n, src, dst, other):
        remote(("t", n), zc, src, dst, ts.at[n], tr.at[n], "mp", other)

    for dy in (2, 1, 3, 0):
        NS[dy] = block(lax.rem(y + dy, NY) * 2 + 1 - core).astype(bf16)
        tsend(dy, NS.at[dy], NR.at[dy], mate)
    for dy in (2, 1, 3, 0):
        N0[dy] = block(ycol(dy))
    zc["t", 2].wait_recv()
    pair = N0[2] + NR[2].astype(f32)
    TS2[0] = pair[:HROW].astype(bf16)
    TS2[1] = pair[HROW:].astype(bf16)
    tsend(4, TS2.at[0], TE.at[0], up)
    tsend(5, TS2.at[1], TE.at[1], down)
    for s, dy, rows, rest in ((0, 1, first, second), (1, 3, second, first)):
        zc["t", dy].wait_recv()
        TS1[s, rest] = (N0[dy, rest] + NR[dy, rest].astype(f32)).astype(bf16)
        zc["t", 4 + s].wait_recv()
        TS1[s, rows] = (
            N0[dy, rows] + NR[dy, rows].astype(f32) + TE[s].astype(f32)
        ).astype(bf16)
        tsend(6 + s, TS1.at[s], TR.at[s], (up, down)[s])
    zc["t", 0].wait_recv()
    zc["t", 6].wait_recv()
    zc["t", 7].wait_recv()
    out[...] = (
        N0[0] + NR[0].astype(f32) + TR[0].astype(f32) + TR[1].astype(f32)
    ).astype(bf16)
    done = {id(xc[l, g, dx]) for l in range(LV) for g in range(5) for dx in range(1, NX)}
    for c in started:
        if id(c) not in done:
            c.wait_send()
    for l in range(LV):
        loc[l, "fresh"].wait()


def step(assign, table, rcp, tokens, cotangent, weights, outer, momentum):
    bf = lambda *shape: pltpu.VMEM(shape, bf16)
    fl = lambda *shape: pltpu.VMEM(shape, f32)
    dense, dense_half = bf(M, B, D), bf(M, B, HALF)
    four, four_half = bf(NX, B, D), bf(NX, B, HALF)
    pairs = lambda kind: [kind] * (2 * LV)
    scratch = [bf(NZ, NX, B, D)] * LV
    for kind in (four_half, four, four_half, dense, dense, dense):
        scratch += pairs(kind)
    for kind in (dense, dense, dense_half, four_half, four_half, four_half, four_half):
        scratch += pairs(kind)
    scratch += [bf(NP, B, D)] * (2 * LV)
    scratch += [fl(M, B, D)] * LV + [dense] * LV
    scratch += [bf(NMP, ROWS, PART)] * 2
    scratch += [fl(NP, B, ROWS)] * 3
    scratch += [bf(NP, B, ROWS)] * 4 + [fl(NP, B, PART), bf(ROWS, HID)]
    scratch += [fl(NY, ROWS, PART), bf(NY, ROWS, PART), bf(NY, ROWS, PART)]
    scratch += [bf(2, HROW, PART)] * 2 + [bf(2, ROWS, PART)] * 2
    scratch += [pltpu.SMEM((LV * NZ * NX * M,), f32)]
    dma = pltpu.SemaphoreType.DMA
    scratch += [dma((2, LV, 5, 3)), dma((2, LV, 5, 3)), dma((LV, 2, 10)), dma((LV, 2, 10))]
    scratch += [dma((20,)), dma((2, 8)), dma((2, 8)), dma((8,)), dma((8,))]
    smem = pl.BlockSpec(memory_space=pltpu.SMEM)
    anyw = pl.BlockSpec(memory_space=pl.ANY)
    return pl.pallas_call(
        step_kernel,
        out_shape=(
            jax.ShapeDtypeStruct((ROWS, PART), bf16),
            jax.ShapeDtypeStruct((LV, M, B, D), bf16),
        ),
        in_specs=[smem, smem, smem, anyw, anyw, anyw, anyw, anyw],
        out_specs=(pl.BlockSpec(memory_space=pltpu.VMEM), anyw),
        scratch_shapes=scratch,
        compiler_params=pltpu.CompilerParams(
            collective_id=0, has_side_effects=True, vmem_limit_bytes=67043328
        ),
    )(assign, table, rcp, tokens, cotangent, weights, outer, momentum)


def shards(tokens, cotangent, path_weights, outer_weights, momentum, assignment, owners):
    here = lax.axis_index("path")
    at_x, at_z = here // NZ, here % NZ
    module_ids = jnp.arange(M, dtype=jnp.int32)
    ids = jnp.arange(NP, dtype=jnp.int32)
    mine = jnp.sum(jnp.where(ids == here, assignment, 0), axis=1)
    rows = jnp.sum(jnp.where((mine[:, None] == module_ids)[:, :, None], owners, 0), axis=1)
    k = (rows % NZ - at_z) % NZ
    place = 2 * (4 - jnp.minimum(k, NZ - k)) - (k < 4).astype(jnp.int32)
    leave = (rows // NZ - at_x) % NX * NZ + place
    back = (at_x - rows // NZ) % NX * NZ + place
    piece = jnp.sum(jnp.where(leave[:, None, :] == ids[:, None], ids, 0), axis=2)
    match = back[2][None, :] == ids[:, None]
    partner = jnp.sum(jnp.where(match[None], back[:2, None, :], 0), axis=2)
    table = jnp.concatenate([piece.reshape(-1), partner.reshape(-1)])
    shares = jnp.sum((assignment[:, None, :] == module_ids[:, None]).astype(f32), axis=2)
    outputs, fresh = step(
        assignment.reshape(-1),
        table,
        (1.0 / shares).reshape(-1),
        tokens,
        cotangent,
        path_weights.reshape(LV, NP, B, D),
        outer_weights.reshape(LV, M, B, D),
        momentum.reshape(LV, M, B, D),
    )
    return (outputs, fresh.reshape(1, LV, M, 1, B, D))


def solution(mesh):
    return jax.shard_map(
        shards,
        mesh=mesh,
        in_specs=(
            P("path", "mp"),
            P("path", "mp"),
            P("path", None, "mp", None),
            P("path", None, None, "mp", None, None),
            P("path", None, None, "mp", None, None),
            P(),
            P(),
        ),
        out_specs=(P("path", "mp"), P("path", None, None, "mp", None, None)),
        check_vma=False,
    )
```

```python
import jax
import jax.numpy as jnp
from jax import lax
from jax.experimental import pallas as pl
from jax.experimental.pallas import tpu as pltpu
from jax.sharding import PartitionSpec as P

MESH = pl.DeviceIdType.MESH
D = 2048
FF = 4096
ROWS = 384
NX = 4
NZ = 8
NY = 4
NP = NX * NZ
NMP = 8
PART = D // NMP
KORD = (4, 3, 5, 2, 6, 1, 7, 0)
POS = {k: i for i, k in enumerate(KORD)}
GROUPS = ((0, 1), (1, 3), (3, 5), (5, 7), (7, 8))
M = 8
LV = 3
B = 16
HID = NP * B
HALF = D // 2
HROW = ROWS // 2
CH = 256
SIGN = (-1, 1)

mu_outer = 0.9
eta_outer = 0.7
lr_inner = 2.0
scale_d = D ** (-0.5)
scale_f = FF ** (-0.5)
f32 = jnp.float32
bf16 = jnp.bfloat16


def contract(left, right, left_dim, right_dim):
    return lax.dot_general(
        left, right, (((left_dim,), (right_dim,)), ((), ())), preferred_element_type=f32
    )


def step_kernel(
    assign, owners, tokens, cotangent, weights, outer, momentum, out, refreshed, *scratch
):
    it = iter(scratch)
    take = lambda n: [next(it) for _ in range(n)]
    pairs = lambda: [take(2) for _ in range(LV)]
    X = take(LV)
    B0, B1o, B1f, T2, B2, B3 = (pairs() for _ in range(6))
    C1, C2, C3d, S2, C3s, S3, C4 = (pairs() for _ in range(7))
    Y, WR, O, F = take(LV), take(LV), take(LV), take(LV)
    xg, cg = take(2)
    A0, A1, A2 = take(3)
    hid, pre0, pre1, perm, G, h2 = take(6)
    N0, NS, NR, TS2, TE, TS1, TR = take(7)
    mask, shares, table = take(3)
    xs, xr, zs, zr, ls, gs, gr, ts, tr = take(9)
    me = lax.axis_index("path")
    mp = lax.axis_index("mp")
    x, z = me // NZ, lax.rem(me, NZ)
    y, core = mp // 2, lax.rem(mp, 2)
    right = [lax.rem(x + dx, NX) * NZ + z for dx in range(NX)]
    along = [x * NZ + lax.rem(z + NZ + s, NZ) for s in SIGN]
    ycol = lambda dy: lax.rem(y + dy + NY, NY) * 2 + core
    up, down, mate = ycol(1), ycol(-1), y * 2 + 1 - core

    barrier = pltpu.get_barrier_semaphore()
    for other in right[1:] + along:
        pl.semaphore_signal(barrier, inc=1, device_id={"path": other}, device_id_type=MESH)
    for other in (up, down, mate):
        pl.semaphore_signal(barrier, inc=1, device_id={"mp": other}, device_id_type=MESH)

    started, zc, xc, loc = [], {}, {}, {}

    def local(key, src, dst, index):
        c = pltpu.make_async_copy(src, dst, ls.at[index])
        c.start()
        loc[key] = c

    def describe(src, dst, ssem, rsem, axis, other):
        return pltpu.make_async_remote_copy(
            src_ref=src, dst_ref=dst, send_sem=ssem, recv_sem=rsem,
            device_id={axis: other}, device_id_type=MESH,
        )

    def remote(key, keep, *rest):
        c = describe(*rest)
        c.start()
        started.append(c)
        keep[key] = c

    local("xg", tokens, xg.at[mp], 15)
    local("cg", cotangent, cg.at[mp], 16)
    for l in range(LV):
        local(("w", l), weights.at[l], WR[l], 12 + l)
        local(("o", l), outer.at[l], O[l], 6 + l)
        local(("v", l), momentum.at[l], F[l], 9 + l)
    pl.semaphore_wait(barrier, 8)

    def gsend(t, n, src, dst, other):
        remote(("g", t, n), zc, src, dst, gs.at[t, n], gr.at[t, n], "mp", other)

    def gwait(t, n, dst):
        describe(dst, dst, gs.at[t, n], gr.at[t, n], "mp", mate).wait_recv()

    both = ((tokens, xg), (cotangent, cg))
    halves = (pl.ds(0, HROW), pl.ds(HROW, HROW))
    lo_y, hi_y, far_y = ycol(-1), ycol(1), ycol(2)

    def offer(t):
        src, g = both[t]
        for n, h in ((0, 0), (8, 1)):
            gsend(t, n, src.at[halves[h]], g.at[mp, halves[h]], up)
            gsend(t, n + 1, src.at[halves[1 - h]], g.at[mp, halves[1 - h]], down)
        gsend(t, 2, src, g.at[mp], mate)

    def relay(t):
        g = both[t][1]
        gwait(t, 0, g.at[lo_y, halves[0]])
        gsend(t, 3, g.at[lo_y, halves[0]], g.at[lo_y, halves[0]], up)
        gwait(t, 1, g.at[hi_y, halves[1]])
        gsend(t, 5, g.at[hi_y, halves[1]], g.at[hi_y, halves[1]], down)

    def share_near(t):
        g = both[t][1]
        gwait(t, 8, g.at[lo_y, halves[1]])
        gsend(t, 4, g.at[lo_y], g.at[lo_y], mate)
        gwait(t, 9, g.at[hi_y, halves[0]])
        gsend(t, 6, g.at[hi_y], g.at[hi_y], mate)

    def share_far(t):
        g = both[t][1]
        gwait(t, 3, g.at[far_y, halves[0]])
        gwait(t, 5, g.at[far_y, halves[1]])
        gsend(t, 7, g.at[far_y], g.at[far_y], mate)

    def near_arrived(t):
        g = both[t][1]
        other = lambda dy: lax.rem(y + dy, NY) * 2 + 1 - core
        loc["xg" if t == 0 else "cg"].wait()
        gwait(t, 2, g.at[other(0)])
        gwait(t, 4, g.at[other(3)])
        gwait(t, 6, g.at[other(1)])

    def far_arrived(t):
        gwait(t, 7, both[t][1].at[lax.rem(y + 2, NY) * 2 + 1 - core])

    def project(acc, w, g, lo=0, hi=NMP):
        def body(i, carry):
            k = i // 2
            dy = k + k // 2 - 2 * (k // 3)
            j = lax.rem(y + dy, NY) * 2 + lax.rem(core + i, 2)
            cols = pl.ds(pl.multiple_of(j * PART, PART), PART)
            part = contract(w[:, :, cols].reshape(HID, PART), g[j], 1, 1)
            acc[...] += part.reshape(NP, B, ROWS)
            return carry

        if lo == 0:
            acc[...] = jnp.zeros_like(acc)
        lax.fori_loop(lo, hi, body, 0)

    def masks(i, carry):
        l, rest = i // (NZ * NX), lax.rem(i, NZ * NX)
        j, r = rest // NX, lax.rem(rest, NX)
        a = assign[l, lax.rem(x - r + NX, NX) * NZ + lax.rem(z + j, NZ)]
        for m in range(M):
            mask[i * M + m] = jnp.where(a == m, 1.0, 0.0).astype(f32)
        return carry

    def count(l):
        def body(p, totals):
            a = assign[l, p]
            return tuple(t + jnp.where(a == m, 1.0, 0.0) for m, t in enumerate(totals))

        totals = lax.fori_loop(0, NP, body, (jnp.float32(0),) * M)
        for m in range(M):
            shares[l * M + m] = totals[m]

    mine = [assign[l, me] for l in range(LV)]

    def pieces(l):
        def body(s, carry):
            dx, i = s // NZ, lax.rem(s, NZ)
            k = 4 + (i + 1) // 2 * (1 - 2 * lax.rem(i, 2))
            path = lax.rem(x + dx, NX) * NZ + lax.rem(z + k, NZ)
            found = jnp.int32(0)
            for q in range(1, NP):
                found = jnp.where(owners[l, mine[l], q] == path, q, found)
            table[l * NP + s] = found
            return carry

        lax.fori_loop(0, NP, body, 0)

    def partners(s, carry):
        r, i = s // NZ, lax.rem(s, NZ)
        q = table[2 * NP + lax.rem(NX - r, NX) * NZ + i]
        for l in (0, 1):
            o = owners[l, mine[l], q]
            k = lax.rem(lax.rem(o, NZ) - z + NZ, NZ)
            i = 2 * (4 - jnp.minimum(k, NZ - k)) - jnp.where(k < 4, 1, 0)
            table[(LV + l) * NP + s] = lax.rem(x - o // NZ + NX, NX) * NZ + i
        return carry

    offer(0)
    lax.fori_loop(0, LV * NZ * NX, masks, 0)
    relay(0)
    offer(1)
    pieces(0)
    share_near(0)
    pieces(1)
    share_far(0)
    relay(1)
    near_arrived(0)
    far_arrived(0)
    loc["w", 0].wait()
    project(A0, WR[0], xg)
    share_near(1)
    loc["w", 1].wait()
    project(A1, WR[1], xg)
    share_far(1)
    near_arrived(1)
    loc["w", 2].wait()
    project(A2, WR[2], cg, 0, 6)
    far_arrived(1)
    project(A2, WR[2], cg, 6, NMP)

    def nonlinear(i, carry):
        gate, upper, back = A0[i] * scale_d, A1[i] * scale_d, A2[i] * scale_f
        sig = jax.nn.sigmoid(gate)
        act = gate * sig
        hid[i] = (act * upper).astype(bf16)
        pre0[i] = (back * upper * sig * (1.0 + gate * (1.0 - sig))).astype(bf16)
        pre1[i] = (back * act).astype(bf16)
        return carry

    lax.fori_loop(0, NP, nonlinear, 0)

    def finals(l, lo, hi):
        left = (pre0, pre1, hid)[l]
        g = (xg, xg, cg)[l]
        rate = lr_inner * (scale_d, scale_d, scale_f)[l]
        n = (hi - lo) * NX

        def slot(i):
            return lax.rem(i, NX) * NZ + i // NX

        def gather(i, carry):
            perm[i] = left[table[l * NP + slot(i)]]
            return carry

        lax.fori_loop(lo * NX, hi * NX, gather, 0, unroll=4)

        def body(j, carry):
            cols = pl.ds(pl.multiple_of(j * PART, PART), PART)
            rows = perm[pl.ds(lo * NX, n)].reshape(n * B, ROWS)
            G[pl.ds(lo * NX, n)] = contract(rows, g[j], 1, 0).reshape(n, B, PART)

            def rows(i, inner):
                s = slot(i)
                w = WR[l][table[l * NP + s], :, cols].astype(f32)
                Y[l][s, :, cols] = (w - rate * G[i]).astype(bf16)
                return inner

            return lax.fori_loop(lo * NX, hi * NX, rows, carry, unroll=4)

        lax.fori_loop(0, NMP, body, 0)

    def zsend(l, s, step, src, dst):
        remote(
            (l, s, step), zc, src, dst, zs.at[l, s, step], zr.at[l, s, step], "path", along[s]
        )

    def zwait(l, s, step):
        zc[l, s, step].wait_recv()

    def xwait(l, g):
        for dx in range(1, NX):
            xc[l, g, dx].wait_recv()

    def combine(dst, bases, terms, lo, hi):
        def body(c, carry):
            col = pl.multiple_of(lo + c * CH, CH)
            vals = [
                (ref[idx, :, pl.ds(pl.multiple_of(col - off, CH), CH)].astype(f32), at)
                for ref, idx, off, at in terms
            ]
            for m in range(M):
                acc = None
                for base in bases:
                    v = base[m, :, pl.ds(col, CH)].astype(f32)
                    acc = v if acc is None else acc + v
                for v, at in vals:
                    t = v * mask[at + m]
                    acc = t if acc is None else acc + t
                dst(m, col, acc)
            return carry

        lax.fori_loop(0, (hi - lo) // CH, body, 0)

    def at(l, j, r):
        return ((l * NZ + j % NZ) * NX + r) * M

    def own(l, k):
        return [(X[l].at[POS[k % NZ]], r, 0, at(l, 0, r)) for r in range(NX)]

    def into(ref):
        def put(m, col, acc):
            ref[m, :, pl.ds(col, CH)] = acc.astype(bf16)
        return put

    def pick(l, j, dx):
        return assign[l, lax.rem(x + dx, NX) * NZ + lax.rem(z + j % NZ, NZ)]

    def send(l, *groups):
        for g in groups:
            lo, hi = GROUPS[g]
            for dx in (1, 3, 2):
                remote(
                    (l, g, dx), xc, Y[l].at[pl.ds(dx * NZ + lo, hi - lo)],
                    X[l].at[pl.ds(lo, hi - lo), dx], xs.at[0, l, g, dx - 1], xr.at[0, l, g, dx - 1],
                    "path", right[dx],
                )

    def keep(l):
        local((l, "own"), Y[l].at[pl.ds(0, NZ)], X[l].at[:, 0], l)

    def a1(l):
        loc[l, "own"].wait()
        xwait(l, 0)
        for s in (0, 1):
            zsend(l, s, 0, X[l].at[0, :, :, pl.ds(s * HALF, HALF)], B0[l][s])

    def a2r(l):
        xwait(l, 1)
        for s in (0, 1):
            zsend(l, s, 1, X[l].at[POS[3 * SIGN[s] % NZ]], B1o[l][s])

    def a2f(l):
        for s in (0, 1):
            zwait(l, s, 0)
            zsend(l, s, 2, B0[l][s], B1f[l][s])

    def near(l, s):
        sg = SIGN[s]
        return own(l, 2 * sg) + [(B1o[l][s], r, 0, at(l, -sg, r)) for r in range(NX)]

    def a3n(l):
        xwait(l, 2)
        for s in (0, 1):
            zwait(l, s, 1)
            o = (1 - s) * HALF
            combine(into(T2[l][s]), [], near(l, s), o, o + HALF)

    def a3f(l):
        for s in (0, 1):
            zwait(l, s, 2)
            o = s * HALF
            far = [(B1f[l][s], r, o, at(l, -2 * SIGN[s], r)) for r in range(NX)]
            combine(into(T2[l][s]), [], near(l, s) + far, o, o + HALF)
            zsend(l, s, 3, T2[l][s], B2[l][s])

    def a4(l):
        xwait(l, 3)
        for s in (0, 1):
            zwait(l, s, 3)
            combine(into(B2[l][s]), [B2[l][s]], own(l, SIGN[s]), 0, D)
            zsend(l, s, 4, B2[l][s], B3[l][s])

    def stage(l, k, src):
        i = POS[k % NZ]
        for dx in range(NX):
            src(dx * NZ + i, dx, pick(l, 0, dx))

    def xsend(l, g):
        lo, hi = GROUPS[g]
        n = hi - lo
        for dx in (1, 3, 2):
            part = pl.ds(dx * NZ + lo, n)
            remote(
                (l, g, dx, "r"), xc, Y[l].at[part], WR[l].at[part],
                xs.at[1, l, g, dx - 1], xr.at[1, l, g, dx - 1], "path", right[dx],
            )

    def a5(l):
        xwait(l, 4)
        loc["o", l].wait()
        loc["v", l].wait()
        for s in (0, 1):
            zwait(l, s, 4)

        def put(m, col, acc):
            cols = pl.ds(col, CH)
            stored = O[l][m, :, cols]
            delta = stored - acc / shares[l * M + m]
            velocity = mu_outer * F[l][m, :, cols].astype(f32) + delta
            F[l][m, :, cols] = (stored - eta_outer * (delta + mu_outer * velocity)).astype(bf16)

        combine(put, [B3[l][0], B3[l][1]], own(l, 0), 0, D)
        for s in (0, 1):
            zsend(l, s, 5, F[l], C1[l][s])
        local((l, "fresh"), F[l], refreshed.at[l], 3 + l)
        for g in range(len(GROUPS)):
            for dx in range(1, NX):
                xc[l, g, dx].wait_send()

        def src(i, dx, a):
            Y[l][i] = F[l][a]

        stage(l, 0, src)
        xsend(l, 4)

    def a6(l):
        for s in (0, 1):
            zwait(l, s, 5)
            zsend(l, s, 6, C1[l][s], C2[l][s])
        for s in (0, 1):
            def src(i, dx, a):
                Y[l][i] = C1[l][s][a]

            stage(l, -SIGN[s], src)
        xsend(l, 3)

    def a7(l):
        for s in (0, 1):
            zwait(l, s, 6)
            zsend(l, s, 7, C2[l][s].at[:, :, pl.ds(s * HALF, HALF)], C3d[l][s])
            for dx in range(NX):
                S2[l][s][dx] = C2[l][s][pick(l, SIGN[s], dx), :, pl.ds((1 - s) * HALF, HALF)]
            zsend(l, s, 8, S2[l][s], C3s[l][s])
        for s in (0, 1):
            def src(i, dx, a):
                Y[l][i] = C2[l][s][a]

            stage(l, -2 * SIGN[s], src)
        xsend(l, 2)

    def a8(l):
        for s in (0, 1):
            zwait(l, s, 7)
            for dx in range(NX):
                S3[l][s][dx] = C3d[l][s][pick(l, SIGN[s], dx)]
            zsend(l, s, 9, S3[l][s], C4[l][s])
        for s in (0, 1):
            zwait(l, s, 8)

            def src(i, dx, a):
                Y[l][i, :, pl.ds(s * HALF, HALF)] = C3d[l][s][a]
                Y[l][i, :, pl.ds((1 - s) * HALF, HALF)] = C3s[l][s][dx]

            stage(l, -3 * SIGN[s], src)
        xsend(l, 1)

    def a9(l):
        for s in (0, 1):
            zwait(l, s, 9)

        def src(i, dx, a):
            for s in (0, 1):
                Y[l][i, :, pl.ds(s * HALF, HALF)] = C4[l][s][dx]

        stage(l, 4, src)
        xsend(l, 0)
        local((l, "mine"), Y[l].at[pl.ds(0, NZ)], WR[l].at[pl.ds(0, NZ)], 17 + l)

    def settle(l):
        for g in range(len(GROUPS)):
            for dx in range(1, NX):
                xc[l, g, dx, "r"].wait_recv()
        loc[l, "mine"].wait()

    def forward(l):
        settle(l)
        if l < 2:
            project((A0, A1)[l], WR[l], xg)
        if l == 1:
            def body(s, carry):
                gate = A0[table[LV * NP + s]] * scale_d
                upper = A1[table[(LV + 1) * NP + s]] * scale_d
                A2[s] = gate * jax.nn.sigmoid(gate) * upper
                return carry

            lax.fori_loop(0, NP, body, 0)
            h2[...] = A2[...].reshape(HID, ROWS).T.astype(bf16)

    finals(0, 0, 1)
    send(0, 0)
    finals(0, 1, NZ)
    send(0, 1, 2)
    keep(0)
    a1(0)
    finals(1, 0, NZ)
    send(1, 0, 1)
    send(0, 3, 4)
    keep(1)
    a2r(0)
    a2f(0)
    pieces(2)
    finals(2, 0, NZ)
    send(1, 2)
    send(2, 0, 1)
    send(1, 3, 4)
    send(2, 2, 3, 4)
    keep(2)
    a3n(0)
    a1(1)
    a3f(0)
    a2r(1)
    a2f(1)
    for l in range(LV):
        count(l)
    lax.fori_loop(0, NP, partners, 0)
    a4(0)
    a3n(1)
    a3f(1)
    a1(2)
    a2r(2)
    a2f(2)
    a5(0)
    a4(1)
    a3n(2)
    a3f(2)
    a6(0)
    a5(1)
    a4(2)
    a7(0)
    a6(1)
    a5(2)
    a8(0)
    a7(1)
    a6(2)
    a9(0)
    a8(1)
    a7(2)
    forward(0)
    a9(1)
    a8(2)
    forward(1)
    a9(2)
    settle(2)

    def block(j):
        cols = pl.ds(pl.multiple_of(j * PART, PART), PART)
        return contract(h2[...], WR[2][:, :, cols].reshape(HID, PART), 1, 0) * scale_f

    def tsend(n, src, dst, other):
        remote(("t", n), zc, src, dst, ts.at[n], tr.at[n], "mp", other)

    for dy in (2, 1, 3, 0):
        NS[dy] = block(lax.rem(y + dy, NY) * 2 + 1 - core).astype(bf16)
        tsend(dy, NS.at[dy], NR.at[dy], mate)
    for dy in (2, 1, 3, 0):
        N0[dy] = block(ycol(dy))
    zc["t", 2].wait_recv()
    pair = N0[2] + NR[2].astype(f32)
    TS2[0] = pair[:HROW].astype(bf16)
    TS2[1] = pair[HROW:].astype(bf16)
    tsend(4, TS2.at[0], TE.at[0], up)
    tsend(5, TS2.at[1], TE.at[1], down)
    for s, dy, rows, rest in ((0, 1, *halves), (1, 3, *halves[::-1])):
        zc["t", dy].wait_recv()
        TS1[s, rest] = (N0[dy, rest] + NR[dy, rest].astype(f32)).astype(bf16)
        zc["t", 4 + s].wait_recv()
        TS1[s, rows] = (
            N0[dy, rows] + NR[dy, rows].astype(f32) + TE[s].astype(f32)
        ).astype(bf16)
        tsend(6 + s, TS1.at[s], TR.at[s], (up, down)[s])
    zc["t", 0].wait_recv()
    zc["t", 6].wait_recv()
    zc["t", 7].wait_recv()
    out[...] = (
        N0[0] + NR[0].astype(f32) + TR[0].astype(f32) + TR[1].astype(f32)
    ).astype(bf16)
    done = {id(xc[l, g, dx]) for l in range(LV) for g in range(5) for dx in range(1, NX)}
    for c in started:
        if id(c) not in done:
            c.wait_send()
    for l in range(LV):
        loc[l, "fresh"].wait()


def step(assign, owners, tokens, cotangent, weights, outer, momentum):
    bf = lambda *shape: pltpu.VMEM(shape, bf16)
    fl = lambda *shape: pltpu.VMEM(shape, f32)
    dense, dense_half = bf(M, B, D), bf(M, B, HALF)
    four, four_half = bf(NX, B, D), bf(NX, B, HALF)
    pairs = lambda kind: [kind] * (2 * LV)
    scratch = [bf(NZ, NX, B, D)] * LV
    for kind in (four_half, four, four_half, dense, dense, dense):
        scratch += pairs(kind)
    for kind in (dense, dense, dense_half, four_half, four_half, four_half, four_half):
        scratch += pairs(kind)
    scratch += [bf(NP, B, D)] * (2 * LV)
    scratch += [fl(M, B, D)] * LV + [dense] * LV
    scratch += [bf(NMP, ROWS, PART)] * 2
    scratch += [fl(NP, B, ROWS)] * 3
    scratch += [bf(NP, B, ROWS)] * 4 + [fl(NP, B, PART), bf(ROWS, HID)]
    scratch += [fl(NY, ROWS, PART), bf(NY, ROWS, PART), bf(NY, ROWS, PART)]
    scratch += [bf(2, HROW, PART)] * 2 + [bf(2, ROWS, PART)] * 2
    scratch += [pltpu.SMEM((LV * NZ * NX * M,), f32), pltpu.SMEM((LV * M,), f32)]
    scratch += [pltpu.SMEM(((LV + 2) * NP,), jnp.int32)]
    dma = pltpu.SemaphoreType.DMA
    scratch += [dma((2, LV, 5, 3)), dma((2, LV, 5, 3)), dma((LV, 2, 10)), dma((LV, 2, 10))]
    scratch += [dma((20,)), dma((2, 10)), dma((2, 10)), dma((8,)), dma((8,))]
    smem = pl.BlockSpec(memory_space=pltpu.SMEM)
    anyw = pl.BlockSpec(memory_space=pl.ANY)
    return pl.pallas_call(
        step_kernel,
        out_shape=(
            jax.ShapeDtypeStruct((ROWS, PART), bf16),
            jax.ShapeDtypeStruct((LV, M, B, D), bf16),
        ),
        in_specs=[smem, smem, anyw, anyw, anyw, anyw, anyw],
        out_specs=(pl.BlockSpec(memory_space=pltpu.VMEM), anyw),
        scratch_shapes=scratch,
        compiler_params=pltpu.CompilerParams(
            collective_id=0, has_side_effects=True, vmem_limit_bytes=67043328
        ),
    )(assign, owners, tokens, cotangent, weights, outer, momentum)


def shards(tokens, cotangent, path_weights, outer_weights, momentum, assignment, owners):
    outputs, fresh = step(
        assignment,
        owners,
        tokens,
        cotangent,
        path_weights.reshape(LV, NP, B, D),
        outer_weights.reshape(LV, M, B, D),
        momentum.reshape(LV, M, B, D),
    )
    return (outputs, fresh.reshape(1, LV, M, 1, B, D))


def solution(mesh):
    return jax.shard_map(
        shards,
        mesh=mesh,
        in_specs=(
            P("path", "mp"),
            P("path", "mp"),
            P("path", None, "mp", None),
            P("path", None, None, "mp", None, None),
            P("path", None, None, "mp", None, None),
            P(),
            P(),
        ),
        out_specs=(P("path", "mp"), P("path", None, None, "mp", None, None)),
        check_vma=False,
    )
```

```python
import jax
import jax.numpy as jnp
from jax import lax
from jax.experimental import pallas as pl
from jax.experimental.pallas import tpu as pltpu
from jax.sharding import PartitionSpec as P

MESH = pl.DeviceIdType.MESH
D = 2048
FF = 4096
ROWS = 384
NX = 4
NZ = 8
NY = 4
NP = NX * NZ
NMP = 8
PART = D // NMP
KORD = (4, 3, 5, 2, 6, 1, 7, 0)
POS = {k: i for i, k in enumerate(KORD)}
GROUPS = ((0, 1), (1, 3), (3, 5), (5, 7), (7, 8))
M = 8
LV = 3
B = 16
HID = NP * B
HALF = D // 2
HROW = ROWS // 2
CH = 256
SIGN = (-1, 1)

mu_outer = 0.9
eta_outer = 0.7
lr_inner = 2.0
scale_d = D ** (-0.5)
scale_f = FF ** (-0.5)
f32 = jnp.float32
bf16 = jnp.bfloat16


def contract(left, right, left_dim, right_dim):
    return lax.dot_general(
        left, right, (((left_dim,), (right_dim,)), ((), ())), preferred_element_type=f32
    )


def step_kernel(
    assign, owners, tokens, cotangent, weights, outer, momentum, out, refreshed, *scratch
):
    it = iter(scratch)
    take = lambda n: [next(it) for _ in range(n)]
    pairs = lambda: [take(2) for _ in range(LV)]
    X = take(LV)
    B0, B1o, B1f, T2, B2, B3 = (pairs() for _ in range(6))
    C1, C2, C3d, S2, C3s, S3, C4 = (pairs() for _ in range(7))
    Y, WR, O, F = take(LV), take(LV), take(LV), take(LV)
    xg, cg = take(2)
    A0, A1, A2 = take(3)
    hid, pre0, pre1, perm, G, h2 = take(6)
    N0, NS, NR, TS2, TE, TS1, TR = take(7)
    mask, shares, table = take(3)
    xs, xr, zs, zr, ls, gs, gr, ts, tr = take(9)
    me = lax.axis_index("path")
    mp = lax.axis_index("mp")
    x, z = me // NZ, lax.rem(me, NZ)
    y, core = mp // 2, lax.rem(mp, 2)
    right = [lax.rem(x + dx, NX) * NZ + z for dx in range(NX)]
    along = [x * NZ + lax.rem(z + NZ + s, NZ) for s in SIGN]
    ycol = lambda dy: lax.rem(y + dy + NY, NY) * 2 + core
    up, down, mate = ycol(1), ycol(-1), y * 2 + 1 - core

    barrier = pltpu.get_barrier_semaphore()
    for other in right[1:] + along:
        pl.semaphore_signal(barrier, inc=1, device_id={"path": other}, device_id_type=MESH)
    for other in (up, down, mate):
        pl.semaphore_signal(barrier, inc=1, device_id={"mp": other}, device_id_type=MESH)

    started, zc, xc, loc = [], {}, {}, {}

    def local(key, src, dst, index):
        c = pltpu.make_async_copy(src, dst, ls.at[index])
        c.start()
        loc[key] = c

    def describe(src, dst, ssem, rsem, axis, other):
        return pltpu.make_async_remote_copy(
            src_ref=src, dst_ref=dst, send_sem=ssem, recv_sem=rsem,
            device_id={axis: other}, device_id_type=MESH,
        )

    def remote(key, keep, *rest):
        c = describe(*rest)
        c.start()
        started.append(c)
        keep[key] = c

    local("xg", tokens, xg.at[mp], 15)
    local("cg", cotangent, cg.at[mp], 16)
    for l in range(LV):
        local(("w", l), weights.at[l], WR[l], 12 + l)
        local(("o", l), outer.at[l], O[l], 6 + l)
        local(("v", l), momentum.at[l], F[l], 9 + l)
    pl.semaphore_wait(barrier, 8)

    def gsend(t, n, src, dst, other):
        remote(("g", t, n), zc, src, dst, gs.at[t, n], gr.at[t, n], "mp", other)

    def gwait(t, n, dst):
        describe(dst, dst, gs.at[t, n], gr.at[t, n], "mp", mate).wait_recv()

    both = ((tokens, xg), (cotangent, cg))
    halves = (pl.ds(0, HROW), pl.ds(HROW, HROW))
    lo_y, hi_y, far_y = ycol(-1), ycol(1), ycol(2)

    def offer(t):
        src, g = both[t]
        for n, h in ((0, 0), (8, 1)):
            gsend(t, n, src.at[halves[h]], g.at[mp, halves[h]], up)
            gsend(t, n + 1, src.at[halves[1 - h]], g.at[mp, halves[1 - h]], down)
        gsend(t, 2, src, g.at[mp], mate)

    def relay(t):
        g = both[t][1]
        gwait(t, 0, g.at[lo_y, halves[0]])
        gsend(t, 3, g.at[lo_y, halves[0]], g.at[lo_y, halves[0]], up)
        gwait(t, 1, g.at[hi_y, halves[1]])
        gsend(t, 5, g.at[hi_y, halves[1]], g.at[hi_y, halves[1]], down)

    def share_near(t):
        g = both[t][1]
        gwait(t, 8, g.at[lo_y, halves[1]])
        gsend(t, 4, g.at[lo_y], g.at[lo_y], mate)
        gwait(t, 9, g.at[hi_y, halves[0]])
        gsend(t, 6, g.at[hi_y], g.at[hi_y], mate)

    def share_far(t):
        g = both[t][1]
        gwait(t, 3, g.at[far_y, halves[0]])
        gwait(t, 5, g.at[far_y, halves[1]])
        gsend(t, 7, g.at[far_y], g.at[far_y], mate)

    def near_arrived(t):
        g = both[t][1]
        other = lambda dy: lax.rem(y + dy, NY) * 2 + 1 - core
        loc["xg" if t == 0 else "cg"].wait()
        gwait(t, 2, g.at[other(0)])
        gwait(t, 4, g.at[other(3)])
        gwait(t, 6, g.at[other(1)])

    def far_arrived(t):
        gwait(t, 7, both[t][1].at[lax.rem(y + 2, NY) * 2 + 1 - core])

    def project(acc, w, g, lo=0, hi=NMP):
        def body(i, carry):
            k = i // 2
            dy = k + k // 2 - 2 * (k // 3)
            j = lax.rem(y + dy, NY) * 2 + lax.rem(core + i, 2)
            cols = pl.ds(pl.multiple_of(j * PART, PART), PART)
            part = contract(w[:, :, cols].reshape(HID, PART), g[j], 1, 1)
            acc[...] += part.reshape(NP, B, ROWS)
            return carry

        if lo == 0:
            acc[...] = jnp.zeros_like(acc)
        lax.fori_loop(lo, hi, body, 0)

    def masks(i, carry):
        l, rest = i // (NZ * NX), lax.rem(i, NZ * NX)
        j, r = rest // NX, lax.rem(rest, NX)
        a = assign[l, lax.rem(x - r + NX, NX) * NZ + lax.rem(z + j, NZ)]
        for m in range(M):
            mask[i * M + m] = jnp.where(a == m, 1.0, 0.0).astype(f32)
        return carry

    def count(l):
        def body(p, totals):
            a = assign[l, p]
            return tuple(t + jnp.where(a == m, 1.0, 0.0) for m, t in enumerate(totals))

        totals = lax.fori_loop(0, NP, body, (jnp.float32(0),) * M)
        for m in range(M):
            shares[l * M + m] = totals[m]

    mine = [assign[l, me] for l in range(LV)]

    def pieces(l):
        def body(s, carry):
            dx, i = s // NZ, lax.rem(s, NZ)
            k = 4 + (i + 1) // 2 * (1 - 2 * lax.rem(i, 2))
            path = lax.rem(x + dx, NX) * NZ + lax.rem(z + k, NZ)
            found = jnp.int32(0)
            for q in range(1, NP):
                found = jnp.where(owners[l, mine[l], q] == path, q, found)
            table[l * NP + s] = found
            return carry

        lax.fori_loop(0, NP, body, 0)

    def partners(s, carry):
        r, i = s // NZ, lax.rem(s, NZ)
        q = table[2 * NP + lax.rem(NX - r, NX) * NZ + i]
        for l in (0, 1):
            o = owners[l, mine[l], q]
            k = lax.rem(lax.rem(o, NZ) - z + NZ, NZ)
            i = 2 * (4 - jnp.minimum(k, NZ - k)) - jnp.where(k < 4, 1, 0)
            table[(LV + l) * NP + s] = lax.rem(x - o // NZ + NX, NX) * NZ + i
        return carry

    offer(0)
    lax.fori_loop(0, LV * NZ * NX, masks, 0)
    relay(0)
    offer(1)
    pieces(0)
    share_near(0)
    pieces(1)
    share_far(0)
    relay(1)
    near_arrived(0)
    far_arrived(0)
    loc["w", 0].wait()
    project(A0, WR[0], xg)
    share_near(1)
    loc["w", 1].wait()
    project(A1, WR[1], xg)
    share_far(1)
    near_arrived(1)
    loc["w", 2].wait()
    project(A2, WR[2], cg, 0, 6)
    far_arrived(1)
    project(A2, WR[2], cg, 6, NMP)

    def nonlinear(i, carry):
        gate, upper, back = A0[i] * scale_d, A1[i] * scale_d, A2[i] * scale_f
        sig = jax.nn.sigmoid(gate)
        act = gate * sig
        hid[i] = (act * upper).astype(bf16)
        pre0[i] = (back * upper * sig * (1.0 + gate * (1.0 - sig))).astype(bf16)
        pre1[i] = (back * act).astype(bf16)
        return carry

    lax.fori_loop(0, NP, nonlinear, 0)

    def finals(l, lo, hi):
        left = (pre0, pre1, hid)[l]
        g = (xg, xg, cg)[l]
        rate = lr_inner * (scale_d, scale_d, scale_f)[l]
        n = (hi - lo) * NX

        def slot(i):
            return lax.rem(i, NX) * NZ + i // NX

        def gather(i, carry):
            perm[i] = left[table[l * NP + slot(i)]]
            return carry

        lax.fori_loop(lo * NX, hi * NX, gather, 0, unroll=4)

        def body(j, carry):
            cols = pl.ds(pl.multiple_of(j * PART, PART), PART)
            rows = perm[pl.ds(lo * NX, n)].reshape(n * B, ROWS)
            G[pl.ds(lo * NX, n)] = contract(rows, g[j], 1, 0).reshape(n, B, PART)

            def rows(i, inner):
                s = slot(i)
                w = WR[l][table[l * NP + s], :, cols].astype(f32)
                Y[l][s, :, cols] = (w - rate * G[i]).astype(bf16)
                return inner

            return lax.fori_loop(lo * NX, hi * NX, rows, carry, unroll=4)

        lax.fori_loop(0, NMP, body, 0)

    def zsend(l, s, step, src, dst):
        remote(
            (l, s, step), zc, src, dst, zs.at[l, s, step], zr.at[l, s, step], "path", along[s]
        )

    def zwait(l, s, step):
        zc[l, s, step].wait_recv()

    def xwait(l, g):
        for dx in range(1, NX):
            xc[l, g, dx].wait_recv()

    def combine(dst, bases, terms, lo, hi):
        def body(c, carry):
            col = pl.multiple_of(lo + c * CH, CH)
            vals = [
                (ref[idx, :, pl.ds(pl.multiple_of(col - off, CH), CH)].astype(f32), at)
                for ref, idx, off, at in terms
            ]
            for m in range(M):
                acc = None
                for base in bases:
                    v = base[m, :, pl.ds(col, CH)].astype(f32)
                    acc = v if acc is None else acc + v
                for v, at in vals:
                    t = v * mask[at + m]
                    acc = t if acc is None else acc + t
                dst(m, col, acc)
            return carry

        lax.fori_loop(0, (hi - lo) // CH, body, 0)

    def at(l, j, r):
        return ((l * NZ + j % NZ) * NX + r) * M

    def own(l, k):
        return [(X[l].at[POS[k % NZ]], r, 0, at(l, 0, r)) for r in range(NX)]

    def into(ref):
        def put(m, col, acc):
            ref[m, :, pl.ds(col, CH)] = acc.astype(bf16)
        return put

    def pick(l, j, dx):
        return assign[l, lax.rem(x + dx, NX) * NZ + lax.rem(z + j % NZ, NZ)]

    def send(l, *groups):
        for g in groups:
            lo, hi = GROUPS[g]
            for dx in (1, 3, 2):
                remote(
                    (l, g, dx), xc, Y[l].at[pl.ds(dx * NZ + lo, hi - lo)],
                    X[l].at[pl.ds(lo, hi - lo), dx], xs.at[0, l, g, dx - 1], xr.at[0, l, g, dx - 1],
                    "path", right[dx],
                )

    def keep(l):
        local((l, "own"), Y[l].at[pl.ds(0, NZ)], X[l].at[:, 0], l)

    def a1(l):
        loc[l, "own"].wait()
        xwait(l, 0)
        for s in (0, 1):
            zsend(l, s, 0, X[l].at[0, :, :, pl.ds(s * HALF, HALF)], B0[l][s])

    def a2r(l):
        xwait(l, 1)
        for s in (0, 1):
            zsend(l, s, 1, X[l].at[POS[3 * SIGN[s] % NZ]], B1o[l][s])

    def a2f(l):
        for s in (0, 1):
            zwait(l, s, 0)
            zsend(l, s, 2, B0[l][s], B1f[l][s])

    def near(l, s):
        sg = SIGN[s]
        return own(l, 2 * sg) + [(B1o[l][s], r, 0, at(l, -sg, r)) for r in range(NX)]

    def a3n(l):
        xwait(l, 2)
        for s in (0, 1):
            zwait(l, s, 1)
            o = (1 - s) * HALF
            combine(into(T2[l][s]), [], near(l, s), o, o + HALF)

    def a3f(l):
        for s in (0, 1):
            zwait(l, s, 2)
            o = s * HALF
            far = [(B1f[l][s], r, o, at(l, -2 * SIGN[s], r)) for r in range(NX)]
            combine(into(T2[l][s]), [], near(l, s) + far, o, o + HALF)
            zsend(l, s, 3, T2[l][s], B2[l][s])

    def a4(l):
        xwait(l, 3)
        for s in (0, 1):
            zwait(l, s, 3)
            combine(into(B2[l][s]), [B2[l][s]], own(l, SIGN[s]), 0, D)
            zsend(l, s, 4, B2[l][s], B3[l][s])

    def stage(l, k, src):
        i = POS[k % NZ]
        for dx in range(NX):
            src(dx * NZ + i, dx, pick(l, 0, dx))

    def xsend(l, g):
        lo, hi = GROUPS[g]
        n = hi - lo
        for dx in (1, 3, 2):
            part = pl.ds(dx * NZ + lo, n)
            remote(
                (l, g, dx, "r"), xc, Y[l].at[part], WR[l].at[part],
                xs.at[1, l, g, dx - 1], xr.at[1, l, g, dx - 1], "path", right[dx],
            )

    def a5(l):
        xwait(l, 4)
        loc["o", l].wait()
        loc["v", l].wait()
        for s in (0, 1):
            zwait(l, s, 4)

        def put(m, col, acc):
            cols = pl.ds(col, CH)
            stored = O[l][m, :, cols]
            delta = stored - acc / shares[l * M + m]
            velocity = mu_outer * F[l][m, :, cols].astype(f32) + delta
            F[l][m, :, cols] = (stored - eta_outer * (delta + mu_outer * velocity)).astype(bf16)

        combine(put, [B3[l][0], B3[l][1]], own(l, 0), 0, D)
        for s in (0, 1):
            zsend(l, s, 5, F[l], C1[l][s])
        local((l, "fresh"), F[l], refreshed.at[l], 3 + l)
        for g in range(len(GROUPS)):
            for dx in range(1, NX):
                xc[l, g, dx].wait_send()

        def src(i, dx, a):
            Y[l][i] = F[l][a]

        stage(l, 0, src)
        xsend(l, 4)

    def a6(l):
        for s in (0, 1):
            zwait(l, s, 5)
            zsend(l, s, 6, C1[l][s], C2[l][s])
        for s in (0, 1):
            def src(i, dx, a):
                Y[l][i] = C1[l][s][a]

            stage(l, -SIGN[s], src)
        xsend(l, 3)

    def a7(l):
        for s in (0, 1):
            zwait(l, s, 6)
            zsend(l, s, 7, C2[l][s].at[:, :, pl.ds(s * HALF, HALF)], C3d[l][s])
            for dx in range(NX):
                S2[l][s][dx] = C2[l][s][pick(l, SIGN[s], dx), :, pl.ds((1 - s) * HALF, HALF)]
            zsend(l, s, 8, S2[l][s], C3s[l][s])
        for s in (0, 1):
            def src(i, dx, a):
                Y[l][i] = C2[l][s][a]

            stage(l, -2 * SIGN[s], src)
        xsend(l, 2)

    def a8(l):
        for s in (0, 1):
            zwait(l, s, 7)
            for dx in range(NX):
                S3[l][s][dx] = C3d[l][s][pick(l, SIGN[s], dx)]
            zsend(l, s, 9, S3[l][s], C4[l][s])
        for s in (0, 1):
            zwait(l, s, 8)

            def src(i, dx, a):
                Y[l][i, :, pl.ds(s * HALF, HALF)] = C3d[l][s][a]
                Y[l][i, :, pl.ds((1 - s) * HALF, HALF)] = C3s[l][s][dx]

            stage(l, -3 * SIGN[s], src)
        xsend(l, 1)

    def a9(l):
        for s in (0, 1):
            zwait(l, s, 9)

        def src(i, dx, a):
            for s in (0, 1):
                Y[l][i, :, pl.ds(s * HALF, HALF)] = C4[l][s][dx]

        stage(l, 4, src)
        xsend(l, 0)
        local((l, "mine"), Y[l].at[pl.ds(0, NZ)], WR[l].at[pl.ds(0, NZ)], 17 + l)

    def settle(l):
        for g in range(len(GROUPS)):
            for dx in range(1, NX):
                xc[l, g, dx, "r"].wait_recv()
        loc[l, "mine"].wait()

    def forward(l):
        settle(l)
        if l < 2:
            project((A0, A1)[l], WR[l], xg)
        if l == 1:
            def body(s, carry):
                gate = A0[table[LV * NP + s]] * scale_d
                upper = A1[table[(LV + 1) * NP + s]] * scale_d
                A2[s] = gate * jax.nn.sigmoid(gate) * upper
                return carry

            lax.fori_loop(0, NP, body, 0)
            h2[...] = A2[...].reshape(HID, ROWS).T.astype(bf16)

    finals(0, 0, 1)
    send(0, 0)
    finals(0, 1, NZ)
    send(0, 1, 2)
    keep(0)
    a1(0)
    finals(1, 0, NZ)
    send(1, 0, 1)
    send(0, 3, 4)
    keep(1)
    a2r(0)
    a2f(0)
    pieces(2)
    finals(2, 0, NZ)
    send(1, 2)
    send(2, 0, 1)
    send(1, 3, 4)
    send(2, 2, 3, 4)
    keep(2)
    a3n(0)
    a1(1)
    a3f(0)
    a2r(1)
    a2f(1)
    for l in range(LV):
        count(l)
    lax.fori_loop(0, NP, partners, 0)
    a4(0)
    a3n(1)
    a3f(1)
    a1(2)
    a2r(2)
    a2f(2)
    a5(0)
    a4(1)
    a3n(2)
    a3f(2)
    a6(0)
    a5(1)
    a4(2)
    a7(0)
    a6(1)
    a5(2)
    a8(0)
    a7(1)
    a6(2)
    a9(0)
    a8(1)
    a7(2)
    forward(0)
    a9(1)
    a8(2)
    a9(2)
    forward(1)
    settle(2)

    def block(j):
        cols = pl.ds(pl.multiple_of(j * PART, PART), PART)
        return contract(h2[...], WR[2][:, :, cols].reshape(HID, PART), 1, 0) * scale_f

    def tsend(n, src, dst, other):
        remote(("t", n), zc, src, dst, ts.at[n], tr.at[n], "mp", other)

    def give(dy):
        NS[dy] = block(lax.rem(y + dy, NY) * 2 + 1 - core).astype(bf16)
        tsend(dy, NS.at[dy], NR.at[dy], mate)

    def hold(dy):
        N0[dy] = block(ycol(dy))

    sides = ((0, 1, *halves), (1, 3, *halves[::-1]))
    for dy in (2, 1, 3):
        give(dy)
    hold(2)
    hold(1)
    zc["t", 2].wait_recv()
    pair = N0[2] + NR[2].astype(f32)
    TS2[0] = pair[:HROW].astype(bf16)
    TS2[1] = pair[HROW:].astype(bf16)
    tsend(4, TS2.at[0], TE.at[0], up)
    tsend(5, TS2.at[1], TE.at[1], down)
    hold(3)
    for s, dy, rows, rest in sides:
        zc["t", dy].wait_recv()
        TS1[s, rest] = (N0[dy, rest] + NR[dy, rest].astype(f32)).astype(bf16)
        tsend(6 + s, TS1.at[s, rest], TR.at[s, rest], (up, down)[s])
    give(0)
    hold(0)
    for s, dy, rows, rest in sides:
        zc["t", 4 + s].wait_recv()
        TS1[s, rows] = (
            N0[dy, rows] + NR[dy, rows].astype(f32) + TE[s].astype(f32)
        ).astype(bf16)
        tsend(8 + s, TS1.at[s, rows], TR.at[s, rows], (up, down)[s])
    for n in (0, 6, 7, 8, 9):
        zc["t", n].wait_recv()
    out[...] = (
        N0[0] + NR[0].astype(f32) + TR[0].astype(f32) + TR[1].astype(f32)
    ).astype(bf16)
    done = {id(xc[l, g, dx]) for l in range(LV) for g in range(5) for dx in range(1, NX)}
    for c in started:
        if id(c) not in done:
            c.wait_send()
    for l in range(LV):
        loc[l, "fresh"].wait()


def step(assign, owners, tokens, cotangent, weights, outer, momentum):
    bf = lambda *shape: pltpu.VMEM(shape, bf16)
    fl = lambda *shape: pltpu.VMEM(shape, f32)
    dense, dense_half = bf(M, B, D), bf(M, B, HALF)
    four, four_half = bf(NX, B, D), bf(NX, B, HALF)
    pairs = lambda kind: [kind] * (2 * LV)
    scratch = [bf(NZ, NX, B, D)] * LV
    for kind in (four_half, four, four_half, dense, dense, dense):
        scratch += pairs(kind)
    for kind in (dense, dense, dense_half, four_half, four_half, four_half, four_half):
        scratch += pairs(kind)
    scratch += [bf(NP, B, D)] * (2 * LV)
    scratch += [fl(M, B, D)] * LV + [dense] * LV
    scratch += [bf(NMP, ROWS, PART)] * 2
    scratch += [fl(NP, B, ROWS)] * 3
    scratch += [bf(NP, B, ROWS)] * 4 + [fl(NP, B, PART), bf(ROWS, HID)]
    scratch += [fl(NY, ROWS, PART), bf(NY, ROWS, PART), bf(NY, ROWS, PART)]
    scratch += [bf(2, HROW, PART)] * 2 + [bf(2, ROWS, PART)] * 2
    scratch += [pltpu.SMEM((LV * NZ * NX * M,), f32), pltpu.SMEM((LV * M,), f32)]
    scratch += [pltpu.SMEM(((LV + 2) * NP,), jnp.int32)]
    dma = pltpu.SemaphoreType.DMA
    scratch += [dma((2, LV, 5, 3)), dma((2, LV, 5, 3)), dma((LV, 2, 10)), dma((LV, 2, 10))]
    scratch += [dma((20,)), dma((2, 10)), dma((2, 10)), dma((10,)), dma((10,))]
    smem = pl.BlockSpec(memory_space=pltpu.SMEM)
    anyw = pl.BlockSpec(memory_space=pl.ANY)
    return pl.pallas_call(
        step_kernel,
        out_shape=(
            jax.ShapeDtypeStruct((ROWS, PART), bf16),
            jax.ShapeDtypeStruct((LV, M, B, D), bf16),
        ),
        in_specs=[smem, smem, anyw, anyw, anyw, anyw, anyw],
        out_specs=(pl.BlockSpec(memory_space=pltpu.VMEM), anyw),
        scratch_shapes=scratch,
        compiler_params=pltpu.CompilerParams(
            collective_id=0, has_side_effects=True, vmem_limit_bytes=67043328
        ),
    )(assign, owners, tokens, cotangent, weights, outer, momentum)


def place_kernel(o, r, out, refreshed, ov, rv, sin, sout):
    parts = [(o, ov, out)] + [(r.at[l], rv.at[l], refreshed.at[l]) for l in range(LV)]
    first = [pltpu.make_async_copy(a, v, sin.at[i]) for i, (a, v, b) in enumerate(parts)]
    last = [pltpu.make_async_copy(v, b, sout.at[i]) for i, (a, v, b) in enumerate(parts)]
    for c in first:
        c.start()
    for c, d in zip(first, last):
        c.wait()
        d.start()
    for d in last:
        d.wait()


def place(o, r):
    anyw = pl.BlockSpec(memory_space=pl.ANY)
    dma = pltpu.SemaphoreType.DMA
    return pl.pallas_call(
        place_kernel,
        out_shape=(jax.ShapeDtypeStruct(o.shape, bf16), jax.ShapeDtypeStruct(r.shape, bf16)),
        in_specs=[anyw, anyw],
        out_specs=(anyw, anyw),
        scratch_shapes=[
            pltpu.VMEM(o.shape, bf16),
            pltpu.VMEM(r.shape, bf16),
            dma((1 + LV,)),
            dma((1 + LV,)),
        ],
    )(o, r)


def shards(tokens, cotangent, path_weights, outer_weights, momentum, assignment, owners):
    outputs, fresh = step(
        assignment,
        owners,
        tokens,
        cotangent,
        path_weights.reshape(LV, NP, B, D),
        outer_weights.reshape(LV, M, B, D),
        momentum.reshape(LV, M, B, D),
    )
    outputs, fresh = place(outputs, fresh)
    return (outputs, fresh.reshape(1, LV, M, 1, B, D))


def solution(mesh):
    return jax.shard_map(
        shards,
        mesh=mesh,
        in_specs=(
            P("path", "mp"),
            P("path", "mp"),
            P("path", None, "mp", None),
            P("path", None, None, "mp", None, None),
            P("path", None, None, "mp", None, None),
            P(),
            P(),
        ),
        out_specs=(P("path", "mp"), P("path", None, None, "mp", None, None)),
        check_vma=False,
    )
```

```python
import jax
import jax.numpy as jnp
from jax import lax
from jax.experimental import pallas as pl
from jax.experimental.pallas import tpu as pltpu
from jax.sharding import PartitionSpec as P

MESH = pl.DeviceIdType.MESH
D = 2048
FF = 4096
ROWS = 384
NX = 4
NZ = 8
NY = 4
NP = NX * NZ
NMP = 8
PART = D // NMP
KORD = (4, 3, 5, 2, 6, 1, 7, 0)
POS = {k: i for i, k in enumerate(KORD)}
GROUPS = ((0, 1), (1, 3), (3, 5), (5, 7), (7, 8))
M = 8
LV = 3
B = 16
HID = NP * B
HALF = D // 2
HROW = ROWS // 2
CH = 256
SIGN = (-1, 1)

mu_outer = 0.9
eta_outer = 0.7
lr_inner = 2.0
scale_d = D ** (-0.5)
scale_f = FF ** (-0.5)
f32 = jnp.float32
bf16 = jnp.bfloat16


def contract(left, right, left_dim, right_dim):
    return lax.dot_general(
        left, right, (((left_dim,), (right_dim,)), ((), ())), preferred_element_type=f32
    )


def step_kernel(
    assign, owners, tokens, cotangent, weights, outer, momentum, out, refreshed, *scratch
):
    it = iter(scratch)
    take = lambda n: [next(it) for _ in range(n)]
    pairs = lambda: [take(2) for _ in range(LV)]
    X = take(LV)
    B0, B1o, B1f, X1o, X1f, T2, B2, B3 = (pairs() for _ in range(8))
    C1, C2, C3d, S2, C3s, S3, C4 = (pairs() for _ in range(7))
    Y, WR, O, F = take(LV), take(LV), take(LV), take(LV)
    xg, cg = take(2)
    A0, A1, A2 = take(3)
    hid, pre0, pre1, perm, G, h2, h2b = take(7)
    N0, N1, NS, NR, TS2, TE, TS1, TR = take(8)
    mask, shares, table = take(3)
    xs, xr, zs, zr, ls, gs, gr, ts, tr = take(9)
    me = lax.axis_index("path")
    mp = lax.axis_index("mp")
    x, z = me // NZ, lax.rem(me, NZ)
    y, core = mp // 2, lax.rem(mp, 2)
    right = [lax.rem(x + dx, NX) * NZ + z for dx in range(NX)]
    along = [x * NZ + lax.rem(z + NZ + s, NZ) for s in SIGN]
    ycol = lambda dy: lax.rem(y + dy + NY, NY) * 2 + core
    up, down, mate = ycol(1), ycol(-1), y * 2 + 1 - core

    barrier = pltpu.get_barrier_semaphore()
    for other in right[1:] + along:
        pl.semaphore_signal(barrier, inc=1, device_id={"path": other}, device_id_type=MESH)
    for other in (up, down, mate):
        pl.semaphore_signal(barrier, inc=1, device_id={"mp": other}, device_id_type=MESH)

    started, zc, xc, loc = [], {}, {}, {}

    def local(key, src, dst, index):
        c = pltpu.make_async_copy(src, dst, ls.at[index])
        c.start()
        loc[key] = c

    def describe(src, dst, ssem, rsem, axis, other):
        return pltpu.make_async_remote_copy(
            src_ref=src, dst_ref=dst, send_sem=ssem, recv_sem=rsem,
            device_id={axis: other}, device_id_type=MESH,
        )

    def remote(key, keep, *rest):
        c = describe(*rest)
        c.start()
        started.append(c)
        keep[key] = c

    local("xg", tokens, xg.at[mp], 15)
    local("cg", cotangent, cg.at[mp], 16)
    for l in range(LV):
        local(("w", l), weights.at[l], WR[l], 12 + l)
        local(("o", l), outer.at[l], O[l], 6 + l)
        local(("v", l), momentum.at[l], F[l], 9 + l)
    pl.semaphore_wait(barrier, 8)

    def gsend(t, n, src, dst, other):
        remote(("g", t, n), zc, src, dst, gs.at[t, n], gr.at[t, n], "mp", other)

    def gwait(t, n, dst):
        describe(dst, dst, gs.at[t, n], gr.at[t, n], "mp", mate).wait_recv()

    both = ((tokens, xg), (cotangent, cg))
    halves = (pl.ds(0, HROW), pl.ds(HROW, HROW))
    lo_y, hi_y, far_y = ycol(-1), ycol(1), ycol(2)

    def offer(t):
        src, g = both[t]
        for n, h in ((0, 0), (8, 1)):
            gsend(t, n, src.at[halves[h]], g.at[mp, halves[h]], up)
            gsend(t, n + 1, src.at[halves[1 - h]], g.at[mp, halves[1 - h]], down)
        gsend(t, 2, src, g.at[mp], mate)

    def relay(t):
        g = both[t][1]
        gwait(t, 0, g.at[lo_y, halves[0]])
        gsend(t, 3, g.at[lo_y, halves[0]], g.at[lo_y, halves[0]], up)
        gwait(t, 1, g.at[hi_y, halves[1]])
        gsend(t, 5, g.at[hi_y, halves[1]], g.at[hi_y, halves[1]], down)

    def share_near(t):
        g = both[t][1]
        gwait(t, 8, g.at[lo_y, halves[1]])
        gsend(t, 4, g.at[lo_y], g.at[lo_y], mate)
        gwait(t, 9, g.at[hi_y, halves[0]])
        gsend(t, 6, g.at[hi_y], g.at[hi_y], mate)

    def share_far(t):
        g = both[t][1]
        gwait(t, 3, g.at[far_y, halves[0]])
        gwait(t, 5, g.at[far_y, halves[1]])
        gsend(t, 7, g.at[far_y], g.at[far_y], mate)

    def near_arrived(t):
        g = both[t][1]
        other = lambda dy: lax.rem(y + dy, NY) * 2 + 1 - core
        loc["xg" if t == 0 else "cg"].wait()
        gwait(t, 2, g.at[other(0)])
        gwait(t, 4, g.at[other(3)])
        gwait(t, 6, g.at[other(1)])

    def far_arrived(t):
        gwait(t, 7, both[t][1].at[lax.rem(y + 2, NY) * 2 + 1 - core])

    def project(acc, w, g, lo=0, hi=NMP):
        def body(i, carry):
            k = i // 2
            dy = k + k // 2 - 2 * (k // 3)
            j = lax.rem(y + dy, NY) * 2 + lax.rem(core + i, 2)
            cols = pl.ds(pl.multiple_of(j * PART, PART), PART)
            part = contract(w[:, :, cols].reshape(HID, PART), g[j], 1, 1)
            acc[...] += part.reshape(NP, B, ROWS)
            return carry

        if lo == 0:
            acc[...] = jnp.zeros_like(acc)
        lax.fori_loop(lo, hi, body, 0)

    def masks(i, carry):
        l, rest = i // (NZ * NX), lax.rem(i, NZ * NX)
        j, r = rest // NX, lax.rem(rest, NX)
        a = assign[l, lax.rem(x - r + NX, NX) * NZ + lax.rem(z + j, NZ)]
        for m in range(M):
            mask[i * M + m] = jnp.where(a == m, 1.0, 0.0).astype(f32)
        return carry

    def count(l):
        def body(p, totals):
            a = assign[l, p]
            return tuple(t + jnp.where(a == m, 1.0, 0.0) for m, t in enumerate(totals))

        totals = lax.fori_loop(0, NP, body, (jnp.float32(0),) * M)
        for m in range(M):
            shares[l * M + m] = totals[m]

    mine = [assign[l, me] for l in range(LV)]

    def pieces(l):
        def body(s, carry):
            dx, i = s // NZ, lax.rem(s, NZ)
            k = 4 + (i + 1) // 2 * (1 - 2 * lax.rem(i, 2))
            path = lax.rem(x + dx, NX) * NZ + lax.rem(z + k, NZ)
            found = jnp.int32(0)
            for q in range(1, NP):
                found = jnp.where(owners[l, mine[l], q] == path, q, found)
            table[l * NP + s] = found
            return carry

        lax.fori_loop(0, NP, body, 0)

    def partners(s, carry):
        r, i = s // NZ, lax.rem(s, NZ)
        q = table[2 * NP + lax.rem(NX - r, NX) * NZ + i]
        for l in (0, 1):
            o = owners[l, mine[l], q]
            k = lax.rem(lax.rem(o, NZ) - z + NZ, NZ)
            i = 2 * (4 - jnp.minimum(k, NZ - k)) - jnp.where(k < 4, 1, 0)
            table[(LV + l) * NP + s] = lax.rem(x - o // NZ + NX, NX) * NZ + i
        return carry

    offer(0)
    lax.fori_loop(0, LV * NZ * NX, masks, 0)
    relay(0)
    offer(1)
    pieces(0)
    share_near(0)
    pieces(1)
    share_far(0)
    relay(1)
    near_arrived(0)
    far_arrived(0)
    loc["w", 0].wait()
    project(A0, WR[0], xg)
    share_near(1)
    loc["w", 1].wait()
    project(A1, WR[1], xg)
    share_far(1)
    near_arrived(1)
    loc["w", 2].wait()
    project(A2, WR[2], cg, 0, 6)
    far_arrived(1)
    project(A2, WR[2], cg, 6, NMP)

    def nonlinear(i, carry):
        gate, upper, back = A0[i] * scale_d, A1[i] * scale_d, A2[i] * scale_f
        sig = jax.nn.sigmoid(gate)
        act = gate * sig
        hid[i] = (act * upper).astype(bf16)
        pre0[i] = (back * upper * sig * (1.0 + gate * (1.0 - sig))).astype(bf16)
        pre1[i] = (back * act).astype(bf16)
        return carry

    lax.fori_loop(0, NP, nonlinear, 0)

    def finals(l, lo, hi):
        left = (pre0, pre1, hid)[l]
        g = (xg, xg, cg)[l]
        rate = lr_inner * (scale_d, scale_d, scale_f)[l]
        n = (hi - lo) * NX

        def slot(i):
            return lax.rem(i, NX) * NZ + i // NX

        def gather(i, carry):
            perm[i] = left[table[l * NP + slot(i)]]
            return carry

        lax.fori_loop(lo * NX, hi * NX, gather, 0, unroll=4)

        def body(j, carry):
            cols = pl.ds(pl.multiple_of(j * PART, PART), PART)
            rows = perm[pl.ds(lo * NX, n)].reshape(n * B, ROWS)
            G[pl.ds(lo * NX, n)] = contract(rows, g[j], 1, 0).reshape(n, B, PART)

            def rows(i, inner):
                s = slot(i)
                w = WR[l][table[l * NP + s], :, cols].astype(f32)
                Y[l][s, :, cols] = (w - rate * G[i]).astype(bf16)
                return inner

            return lax.fori_loop(lo * NX, hi * NX, rows, carry, unroll=4)

        lax.fori_loop(0, NMP, body, 0)

    def zsend(l, s, step, src, dst):
        remote(
            (l, s, step), zc, src, dst, zs.at[l, s, step], zr.at[l, s, step], "path", along[s]
        )

    def zwait(l, s, step):
        zc[l, s, step].wait_recv()

    def xwait(l, g):
        for dx in range(1, NX):
            xc[l, g, dx].wait_recv()

    def combine(dst, bases, terms, lo, hi):
        def body(c, carry):
            col = pl.multiple_of(lo + c * CH, CH)
            vals = [
                (ref[idx, :, pl.ds(pl.multiple_of(col - off, CH), CH)].astype(f32), at)
                for ref, idx, off, at in terms
            ]
            for m in range(M):
                acc = None
                for base in bases:
                    v = base[m, :, pl.ds(col, CH)].astype(f32)
                    acc = v if acc is None else acc + v
                for v, at in vals:
                    t = v * mask[at + m]
                    acc = t if acc is None else acc + t
                dst(m, col, acc)
            return carry

        lax.fori_loop(0, (hi - lo) // CH, body, 0)

    def at(l, j, r):
        return ((l * NZ + j % NZ) * NX + r) * M

    def own(l, k):
        return [(X[l].at[POS[k % NZ] - 3], r, 0, at(l, 0, r)) for r in range(NX)]

    def into(ref):
        def put(m, col, acc):
            ref[m, :, pl.ds(col, CH)] = acc.astype(bf16)
        return put

    def pick(l, j, dx):
        return assign[l, lax.rem(x + dx, NX) * NZ + lax.rem(z + j % NZ, NZ)]

    def send(l, *groups):
        for g in groups:
            lo, hi = GROUPS[g]
            for dx in (1, 3, 2):
                remote(
                    (l, g, dx), xc, Y[l].at[pl.ds(dx * NZ + lo, hi - lo)],
                    X[l].at[pl.ds(lo - 3, hi - lo), dx], xs.at[0, l, g, dx - 1], xr.at[0, l, g, dx - 1],
                    "path", right[dx],
                )

    def keep(l):
        local((l, "own"), Y[l].at[pl.ds(3, NZ - 3)], X[l].at[:, 0], l)

    def early4(l):
        for dx in range(NX):
            for s in (0, 1):
                half = pl.ds(s * HALF, HALF)
                zsend(l, s, 10 + dx, Y[l].at[dx * NZ, :, half], B0[l][s].at[dx])

    def early3(l):
        for dx in range(NX):
            for s in (0, 1):
                zsend(l, s, 14 + dx, Y[l].at[dx * NZ + POS[3 * SIGN[s] % NZ]], B1o[l][s].at[dx])

    def a2f(l):
        for s in (0, 1):
            for dx in range(NX):
                zwait(l, s, 10 + dx)
            zsend(l, s, 2, B0[l][s], B1f[l][s])

    def axn(l):
        for s in (0, 1):
            for dx in range(NX):
                zwait(l, s, 14 + dx)
            for dx in (1, 3, 2):
                remote(
                    (l, "o", s, dx), xc, B1o[l][s].at[dx], X1o[l][s].at[dx],
                    xs.at[0, l, s, dx - 1], xr.at[0, l, s, dx - 1], "path", right[dx],
                )

    def axf(l):
        for s in (0, 1):
            zwait(l, s, 2)
            for dx in (1, 3, 2):
                remote(
                    (l, "f", s, dx), xc, B1f[l][s].at[dx], X1f[l][s].at[dx],
                    xs.at[2, l, s, dx - 1], xr.at[2, l, s, dx - 1], "path", right[dx],
                )

    def near(l, s):
        sg = SIGN[s]
        terms = [(B1o[l][s], 0, 0, at(l, -sg, 0))]
        terms += [(X1o[l][s], r, 0, at(l, -sg, r)) for r in range(1, NX)]
        return own(l, 2 * sg) + terms

    def a3n(l):
        loc[l, "own"].wait()
        xwait(l, 2)
        for s in (0, 1):
            for dx in range(1, NX):
                xc[l, "o", s, dx].wait_recv()
            o = (1 - s) * HALF
            combine(into(T2[l][s]), [], near(l, s), o, o + HALF)

    def a3f(l):
        for s in (0, 1):
            for dx in range(1, NX):
                xc[l, "f", s, dx].wait_recv()
            o = s * HALF
            far = [(B1f[l][s], 0, o, at(l, -2 * SIGN[s], 0))]
            far += [(X1f[l][s], r, o, at(l, -2 * SIGN[s], r)) for r in range(1, NX)]
            combine(into(T2[l][s]), [], near(l, s) + far, o, o + HALF)
            zsend(l, s, 3, T2[l][s], B2[l][s])

    def a4(l):
        xwait(l, 3)
        for s in (0, 1):
            zwait(l, s, 3)
            combine(into(B2[l][s]), [B2[l][s]], own(l, SIGN[s]), 0, D)
            zsend(l, s, 4, B2[l][s], B3[l][s])

    def stage(l, k, src):
        i = POS[k % NZ]
        for dx in range(NX):
            src(dx * NZ + i, dx, pick(l, 0, dx))

    def xsend(l, g):
        lo, hi = GROUPS[g]
        n = hi - lo
        for dx in (1, 3, 2):
            part = pl.ds(dx * NZ + lo, n)
            remote(
                (l, g, dx, "r"), xc, Y[l].at[part], WR[l].at[part],
                xs.at[1, l, g, dx - 1], xr.at[1, l, g, dx - 1], "path", right[dx],
            )

    def a5(l):
        xwait(l, 4)
        loc["o", l].wait()
        loc["v", l].wait()
        for s in (0, 1):
            zwait(l, s, 4)

        def put(m, col, acc):
            cols = pl.ds(col, CH)
            stored = O[l][m, :, cols]
            delta = stored - acc / shares[l * M + m]
            velocity = mu_outer * F[l][m, :, cols].astype(f32) + delta
            F[l][m, :, cols] = (stored - eta_outer * (delta + mu_outer * velocity)).astype(bf16)

        combine(put, [B3[l][0], B3[l][1]], own(l, 0), 0, D)
        for s in (0, 1):
            zsend(l, s, 5, F[l], C1[l][s])
        local((l, "fresh"), F[l], refreshed.at[l], 3 + l)
        for g in range(2, len(GROUPS)):
            for dx in range(1, NX):
                xc[l, g, dx].wait_send()
        for s in (0, 1):
            for n in range(10, 18):
                zc[l, s, n].wait_send()

        def src(i, dx, a):
            Y[l][i] = F[l][a]

        stage(l, 0, src)
        xsend(l, 4)

    def a6(l):
        for s in (0, 1):
            zwait(l, s, 5)
            zsend(l, s, 6, C1[l][s], C2[l][s])
        for s in (0, 1):
            def src(i, dx, a):
                Y[l][i] = C1[l][s][a]

            stage(l, -SIGN[s], src)
        xsend(l, 3)

    def a7(l):
        for s in (0, 1):
            zwait(l, s, 6)
            zsend(l, s, 7, C2[l][s].at[:, :, pl.ds(s * HALF, HALF)], C3d[l][s])
            for dx in range(NX):
                S2[l][s][dx] = C2[l][s][pick(l, SIGN[s], dx), :, pl.ds((1 - s) * HALF, HALF)]
            zsend(l, s, 8, S2[l][s], C3s[l][s])
        for s in (0, 1):
            def src(i, dx, a):
                Y[l][i] = C2[l][s][a]

            stage(l, -2 * SIGN[s], src)
        xsend(l, 2)

    def a8(l):
        for s in (0, 1):
            zwait(l, s, 7)
            for dx in range(NX):
                S3[l][s][dx] = C3d[l][s][pick(l, SIGN[s], dx)]
            zsend(l, s, 9, S3[l][s], C4[l][s])
        for s in (0, 1):
            zwait(l, s, 8)

            def src(i, dx, a):
                Y[l][i, :, pl.ds(s * HALF, HALF)] = C3d[l][s][a]
                Y[l][i, :, pl.ds((1 - s) * HALF, HALF)] = C3s[l][s][dx]

            stage(l, -3 * SIGN[s], src)
        xsend(l, 1)

    def a9(l):
        for s in (0, 1):
            zwait(l, s, 9)

        def src(i, dx, a):
            for s in (0, 1):
                Y[l][i, :, pl.ds(s * HALF, HALF)] = C4[l][s][dx]

        stage(l, 4, src)
        xsend(l, 0)
        local((l, "mine"), Y[l].at[pl.ds(0, NZ)], WR[l].at[pl.ds(0, NZ)], 17 + l)

    def settle(l, first=0, last=len(GROUPS)):
        for g in range(first, last):
            for dx in range(1, NX):
                xc[l, g, dx, "r"].wait_recv()
        if last == len(GROUPS):
            loc[l, "mine"].wait()

    def forward(l):
        settle(l)
        if l < 2:
            project((A0, A1)[l], WR[l], xg)
        if l == 1:
            def unit(i, s):
                gate = A0[table[LV * NP + s]] * scale_d
                upper = A1[table[(LV + 1) * NP + s]] * scale_d
                A2[i] = gate * jax.nn.sigmoid(gate) * upper

            def body(i, carry):
                unit(i, i // (NZ - 1) * NZ + 1 + lax.rem(i, NZ - 1))
                return carry

            lax.fori_loop(0, NP - NX, body, 0)
            for dx in range(NX):
                unit(NP - NX + dx, dx * NZ)
            h2[...] = A2[: NP - NX].reshape(HID - NX * B, ROWS).T.astype(bf16)
            h2b[...] = A2[NP - NX :].reshape(NX * B, ROWS).T.astype(bf16)

    finals(0, 0, 1)
    early4(0)
    finals(0, 1, NZ)
    early3(0)
    send(0, 2)
    keep(0)
    a2f(0)
    finals(1, 0, NZ)
    early4(1)
    early3(1)
    keep(1)
    axn(0)
    pieces(2)
    axf(0)
    send(0, 3)
    send(1, 2)
    finals(2, 0, NZ)
    keep(2)
    a2f(1)
    a3n(0)
    axn(1)
    a3f(0)
    early4(2)
    early3(2)
    axf(1)
    send(0, 4)
    send(1, 3)
    send(2, 2)
    for l in range(LV):
        count(l)
    lax.fori_loop(0, NP, partners, 0)
    a4(0)
    a2f(2)
    a3n(1)
    a3f(1)
    axn(2)
    axf(2)
    send(1, 4)
    send(2, 3, 4)
    a5(0)
    a4(1)
    a3n(2)
    a3f(2)
    a6(0)
    a5(1)
    a4(2)
    a7(0)
    a6(1)
    a5(2)
    a8(0)
    a7(1)
    a6(2)
    a9(0)
    a8(1)
    a7(2)
    forward(0)
    a9(1)
    a8(2)
    a9(2)
    forward(1)
    settle(2, 1)

    def columns(j):
        return pl.ds(pl.multiple_of(j * PART, PART), PART)

    def mate_col(dy):
        return lax.rem(y + dy, NY) * 2 + 1 - core

    def most(j):
        rows = [
            WR[2][pl.ds(dx * NZ + 1, NZ - 1), :, columns(j)].reshape((NZ - 1) * B, PART)
            for dx in range(NX)
        ]
        return contract(h2[...], jnp.concatenate(rows, axis=0), 1, 0)

    def rest_of(j):
        rows = [WR[2][dx * NZ, :, columns(j)] for dx in range(NX)]
        return contract(h2b[...], jnp.concatenate(rows, axis=0), 1, 0)

    def partials(dy, carry):
        N1[dy] = most(mate_col(dy))
        N0[dy] = most(ycol(dy))
        return carry

    lax.fori_loop(0, NY, partials, 0)
    settle(2, 0, 1)

    def tsend(n, src, dst, other):
        remote(("t", n), zc, src, dst, ts.at[n], tr.at[n], "mp", other)

    def give(dy):
        NS[dy] = ((N1[dy] + rest_of(mate_col(dy))) * scale_f).astype(bf16)
        tsend(dy, NS.at[dy], NR.at[dy], mate)

    def hold(dy):
        N0[dy] = (N0[dy] + rest_of(ycol(dy))) * scale_f

    sides = ((0, 1, *halves), (1, 3, *halves[::-1]))
    for dy in (2, 1, 3):
        give(dy)
    hold(2)
    hold(1)
    zc["t", 2].wait_recv()
    pair = N0[2] + NR[2].astype(f32)
    TS2[0] = pair[:HROW].astype(bf16)
    TS2[1] = pair[HROW:].astype(bf16)
    tsend(4, TS2.at[0], TE.at[0], up)
    tsend(5, TS2.at[1], TE.at[1], down)
    hold(3)
    for s, dy, rows, rest in sides:
        zc["t", dy].wait_recv()
        TS1[s, rest] = (N0[dy, rest] + NR[dy, rest].astype(f32)).astype(bf16)
        tsend(6 + s, TS1.at[s, rest], TR.at[s, rest], (up, down)[s])
    give(0)
    hold(0)
    for s, dy, rows, rest in sides:
        zc["t", 4 + s].wait_recv()
        TS1[s, rows] = (
            N0[dy, rows] + NR[dy, rows].astype(f32) + TE[s].astype(f32)
        ).astype(bf16)
        tsend(8 + s, TS1.at[s, rows], TR.at[s, rows], (up, down)[s])
    for n in (0, 6, 7, 8, 9):
        zc["t", n].wait_recv()
    out[...] = (
        N0[0] + NR[0].astype(f32) + TR[0].astype(f32) + TR[1].astype(f32)
    ).astype(bf16)
    done = {id(xc[l, g, dx]) for l in range(LV) for g in range(2, 5) for dx in range(1, NX)}
    done |= {id(zc[l, s, n]) for l in range(LV) for s in (0, 1) for n in range(10, 18)}
    for c in started:
        if id(c) not in done:
            c.wait_send()
    for l in range(LV):
        loc[l, "fresh"].wait()


def step(assign, owners, tokens, cotangent, weights, outer, momentum):
    bf = lambda *shape: pltpu.VMEM(shape, bf16)
    fl = lambda *shape: pltpu.VMEM(shape, f32)
    dense, dense_half = bf(M, B, D), bf(M, B, HALF)
    four, four_half = bf(NX, B, D), bf(NX, B, HALF)
    pairs = lambda kind: [kind] * (2 * LV)
    scratch = [bf(NZ - 3, NX, B, D)] * LV
    for kind in (four_half, four, four_half, four, four_half, dense, dense, dense):
        scratch += pairs(kind)
    for kind in (dense, dense, dense_half, four_half, four_half, four_half, four_half):
        scratch += pairs(kind)
    scratch += [bf(NP, B, D)] * (2 * LV)
    scratch += [fl(M, B, D)] * LV + [dense] * LV
    scratch += [bf(NMP, ROWS, PART)] * 2
    scratch += [fl(NP, B, ROWS)] * 3
    scratch += [bf(NP, B, ROWS)] * 4 + [fl(NP, B, PART), bf(ROWS, HID - NX * B), bf(ROWS, NX * B)]
    scratch += [fl(NY, ROWS, PART), fl(NY, ROWS, PART), bf(NY, ROWS, PART), bf(NY, ROWS, PART)]
    scratch += [bf(2, HROW, PART)] * 2 + [bf(2, ROWS, PART)] * 2
    scratch += [pltpu.SMEM((LV * NZ * NX * M,), f32), pltpu.SMEM((LV * M,), f32)]
    scratch += [pltpu.SMEM(((LV + 2) * NP,), jnp.int32)]
    dma = pltpu.SemaphoreType.DMA
    scratch += [dma((3, LV, 5, 3)), dma((3, LV, 5, 3)), dma((LV, 2, 18)), dma((LV, 2, 18))]
    scratch += [dma((20,)), dma((2, 10)), dma((2, 10)), dma((10,)), dma((10,))]
    smem = pl.BlockSpec(memory_space=pltpu.SMEM)
    anyw = pl.BlockSpec(memory_space=pl.ANY)
    return pl.pallas_call(
        step_kernel,
        out_shape=(
            jax.ShapeDtypeStruct((ROWS, PART), bf16),
            jax.ShapeDtypeStruct((LV, M, B, D), bf16),
        ),
        in_specs=[smem, smem, anyw, anyw, anyw, anyw, anyw],
        out_specs=(pl.BlockSpec(memory_space=pltpu.VMEM), anyw),
        scratch_shapes=scratch,
        compiler_params=pltpu.CompilerParams(
            collective_id=0, has_side_effects=True, vmem_limit_bytes=67043328
        ),
    )(assign, owners, tokens, cotangent, weights, outer, momentum)


def place_kernel(o, r, out, refreshed, ov, rv, sin, sout):
    parts = [(o, ov, out)] + [(r.at[l], rv.at[l], refreshed.at[l]) for l in range(LV)]
    first = [pltpu.make_async_copy(a, v, sin.at[i]) for i, (a, v, b) in enumerate(parts)]
    last = [pltpu.make_async_copy(v, b, sout.at[i]) for i, (a, v, b) in enumerate(parts)]
    for c in first:
        c.start()
    for c, d in zip(first, last):
        c.wait()
        d.start()
    for d in last:
        d.wait()


def place(o, r):
    anyw = pl.BlockSpec(memory_space=pl.ANY)
    dma = pltpu.SemaphoreType.DMA
    return pl.pallas_call(
        place_kernel,
        out_shape=(jax.ShapeDtypeStruct(o.shape, bf16), jax.ShapeDtypeStruct(r.shape, bf16)),
        in_specs=[anyw, anyw],
        out_specs=(anyw, anyw),
        scratch_shapes=[
            pltpu.VMEM(o.shape, bf16),
            pltpu.VMEM(r.shape, bf16),
            dma((1 + LV,)),
            dma((1 + LV,)),
        ],
    )(o, r)


def shards(tokens, cotangent, path_weights, outer_weights, momentum, assignment, owners):
    outputs, fresh = step(
        assignment,
        owners,
        tokens,
        cotangent,
        path_weights.reshape(LV, NP, B, D),
        outer_weights.reshape(LV, M, B, D),
        momentum.reshape(LV, M, B, D),
    )
    outputs, fresh = place(outputs, fresh)
    return (outputs, fresh.reshape(1, LV, M, 1, B, D))


def solution(mesh):
    return jax.shard_map(
        shards,
        mesh=mesh,
        in_specs=(
            P("path", "mp"),
            P("path", "mp"),
            P("path", None, "mp", None),
            P("path", None, None, "mp", None, None),
            P("path", None, None, "mp", None, None),
            P(),
            P(),
        ),
        out_specs=(P("path", "mp"), P("path", None, None, "mp", None, None)),
        check_vma=False,
    )
```
